32 devices in a mesh: grp: 2 (over y), blk: 4 (over z), bulk: 4 (over x, core).
Axes of the slice: x: 2, y: 2, z: 4, core: 2. Of those that a mesh axis runs over, the one named last changes fastest.
Arguments:
- tokens: bfloat16 [80, 8192], P(('grp', 'blk'), 'bulk'), parts along dimension 0, may hold values from -6 to 6
- cotangent: bfloat16 [80, 8192], P(('grp', 'blk'), 'bulk'), parts along dimension 0, may hold values from -1.5 to 1.5
- gate_weight: bfloat16 [8192, 26624], P('bulk', 'blk'), may hold values from -0.0625 to 0.0625
- up_weight: bfloat16 [8192, 26624], P('bulk', 'blk'), may hold values from -0.0625 to 0.0625
- down_weight: bfloat16 [26624, 8192], P('blk', 'bulk'), may hold values from -0.0390625 to 0.0390625
Outputs:
- mixed: bfloat16 [80, 8192], P(('grp', 'blk'), 'bulk'), parts along dimension 0
- grad_input: bfloat16 [80, 8192], P(('grp', 'blk'), 'bulk'), parts along dimension 0
The draws below stay inside these ranges and needn't reach their ends.
There are 2 independent parts, one for each index of `grp`. The reference program is written for one: setup_inputs(seed, part) draws one part's arguments, and reference() takes and returns one part's arrays. A program takes and returns all parts, laid end to end along the dimension named above; an argument that names none is the same for every part. Nothing has to cross between parts.
All inputs are finite; a program needn't handle non-finite values.
Results may differ from the reference program's by a relative error of at most 0.0049.
Values may be sent and summed in bfloat16 or wider, within the bound.
A program may use at most 192 MiB of HBM per device.

```python
import jax
import jax.numpy as jnp
from jax import lax

D = 8192
FF = 26624
TOKENS = 40


def levels(rng, dims, split, low, largest):
    def one(position, shards_of):
        draws = jax.random.uniform(jax.random.fold_in(jax.random.fold_in(rng, 6), position), (shards_of,), jnp.float32, low / len(split), largest / len(split))
        return jnp.repeat(jnp.exp(draws), dims[position] // shards_of).reshape((-1,) + (1,) * (len(dims) - position - 1))

    loudness = one(*split[0])
    for cut in split[1:]:
        loudness = loudness * one(*cut)
    return loudness


def normal_values(stream_key, extent, scale, reach, cuts=(), dtype=jnp.bfloat16):
    gain = levels(stream_key, extent, cuts, -0.22, 0.18) if cuts else 1.0
    values = jax.random.normal(stream_key, extent, jnp.float32) * scale * gain
    return jnp.minimum(jnp.maximum(values, -reach), reach).astype(dtype)


def setup_inputs(seed: int = 0, part: int = 0) -> dict:
    seeds = jax.random.split(jax.random.key(seed), 6)
    own_keys = jax.random.split(jax.random.fold_in(seeds[5], part), 6)
    tokens = normal_values(own_keys[0], (TOKENS, D), 1.0, 6.0, ((0, 4), (1, 4)))
    cotangent = normal_values(own_keys[1], (TOKENS, D), 0.25, 1.5, ((0, 4), (1, 4)))
    gate_weight = normal_values(seeds[2], (D, FF), D ** -0.5, 0.0625, ((0, 4), (1, 4)))
    up_weight = normal_values(seeds[3], (D, FF), D ** -0.5, 0.0625, ((0, 4), (1, 4)))
    down_weight = normal_values(seeds[4], (FF, D), FF ** -0.5, 0.0390625, ((0, 4), (1, 4)))
    return {"tokens": tokens, "cotangent": cotangent, "gate_weight": gate_weight, "up_weight": up_weight, "down_weight": down_weight}


def reference(tokens, cotangent, gate_weight, up_weight, down_weight):
    gate = jnp.dot(tokens, gate_weight, preferred_element_type=jnp.float32)
    upward = jnp.dot(tokens, up_weight, preferred_element_type=jnp.float32)
    sigma = jax.nn.sigmoid(gate)
    hidden = (gate * sigma * upward).astype(jnp.bfloat16)
    mixed = jnp.dot(hidden, down_weight, preferred_element_type=jnp.float32).astype(jnp.bfloat16)
    back = lax.dot_general(cotangent, down_weight, (((1,), (1,)), ((), ())), preferred_element_type=jnp.float32)
    d_up = (back * gate * sigma).astype(jnp.bfloat16)
    d_gate = (back * upward * sigma * (1.0 + gate * (1.0 - sigma))).astype(jnp.bfloat16)
    first_part = lax.dot_general(d_gate, gate_weight, (((1,), (1,)), ((), ())), preferred_element_type=jnp.float32)
    second_part = lax.dot_general(d_up, up_weight, (((1,), (1,)), ((), ())), preferred_element_type=jnp.float32)
    grad_input = (first_part + second_part).astype(jnp.bfloat16)
    return mixed, grad_input
```

```python
import functools

import jax
import jax.numpy as jnp
from jax import lax
from jax.experimental import pallas as pl
from jax.experimental.pallas import tpu as pltpu
from jax.sharding import PartitionSpec as P

MESH = pl.DeviceIdType.MESH
BF = jnp.bfloat16
F32 = jnp.float32
NT = (((1,), (1,)), ((), ()))
EARLY = 4
PARTS = 4


def flip(i, m):
    return i + m - 2 * m * ((i // m) % 2)


def kernel(nb, nu, n, total, fc, tok_in, cot_in, wg_hbm, wu_hbm, wd_hbm, out,
           wg, wu, wd, got, tok, cot, part, pair, chip, far, coef, act,
           mixed, grad, ysend, yrecv, ysum, zsend, zrecv,
           g_sem, u_sem, d_sem, own_sem, tk_send, tk_recv, p_send, p_recv,
           f_send, f_recv, a_send, a_recv, y_send, y_recv, z_send, z_recv):
    g_me = lax.axis_index("grp")
    b_me = lax.axis_index("blk")
    u_me = lax.axis_index("bulk")
    x_me, k_me = u_me // 2, u_me % 2
    chips = nu // 2
    rows, depth = tok_in.shape
    half = nb * rows
    pw = depth // PARTS
    steps = nb.bit_length() - 1
    bits = [1 << s for s in range(steps)]
    first_chunk = jnp.minimum(g_me * n, total - n)
    partner = {"bulk": x_me * 2 + (1 - k_me)}
    across = {"grp": 1 - g_me}

    def zpeer(m):
        return {"blk": flip(b_me, m)}

    def xpeer(d):
        return {"bulk": ((x_me + d) % chips) * 2 + k_me}

    def rcopy(src, dst, ss, rs, where):
        return pltpu.make_async_remote_copy(
            src_ref=src, dst_ref=dst, send_sem=ss, recv_sem=rs, device_id=where, device_id_type=MESH)


    def load_gu(c):
        cols = pl.ds(pl.multiple_of((first_chunk + c) * fc, fc), fc)
        return (pltpu.make_async_copy(wg_hbm.at[:, cols], wg.at[c], g_sem.at[c]),
                pltpu.make_async_copy(wu_hbm.at[:, cols], wu.at[c], u_sem.at[c]))

    def load_d(c):
        rws = pl.ds(pl.multiple_of((first_chunk + c) * fc, fc), fc)
        return pltpu.make_async_copy(wd_hbm.at[rws, :], wd.at[c], d_sem.at[c])


    dims = bits[::-1] + [nb]

    def across_dim(m):
        return across if m == nb else zpeer(m)

    def tok_copy(w, e, m):
        src = (tok_in, cot_in)[w] if e == 0 else got.at[w, e]
        i = dims.index(m)
        return rcopy(src, got.at[w, e + m], tk_send.at[w, e, i], tk_recv.at[w, e + m], across_dim(m))

    def later(e):
        last = max([i for i, m in enumerate(dims) if (e // m) % 2], default=-1)
        return dims[last + 1:]

    def tok_forward(w, e):
        if e:
            rcopy(got.at[w, e], got.at[w, e], tk_send.at[w, e, 0], tk_recv.at[w, e], across).wait_recv()
        for m in later(e):
            tok_copy(w, e, m).start()

    def own_copy(w):
        return pltpu.make_async_copy((tok_in, cot_in)[w], got.at[w, 0], own_sem.at[w])

    def pack(w, scratch, dst):
        for e in range(2 * nb):
            if e >= nb:
                tok_forward(w, e)
            if e == 0:
                own_copy(w).wait()
            scratch[e * rows:(e + 1) * rows, :] = got[w, e].astype(F32)
        dst[...] = scratch[...].astype(BF)


    def js(t):
        return pl.ds(0, 2) if t == 0 else pl.ds(2, 1)

    def pair_copy(t, c):
        return rcopy(part.at[c, 1 - k_me, js(t)], pair.at[c, js(t)], p_send.at[t, c], p_recv.at[t, c], partner)

    def chip_sum(t, c):
        pair_copy(t, c).wait_recv()
        for j in ((0, 1), (2,))[t]:
            chip[c, j] = (part[c, k_me, j] + pair[c, j]).astype(BF)

    def far_copy(t, c, d):
        return rcopy(chip.at[c, js(t)], far.at[c, d - 1, js(t)], f_send.at[t, c, d - 1], f_recv.at[t, c, d - 1],
                     xpeer(d))

    def far_start(t, c):
        for d in range(1, chips):
            far_copy(t, c, d).start()

    def activate(t, c):
        for d in range(1, chips):
            far_copy(t, c, d).wait_recv()

        def total_of(j):
            s = part[c, k_me, j] + pair[c, j]
            for d in range(1, chips):
                s = s + far[c, d - 1, j].astype(F32)
            return s

        if t == 0:
            gate, upward = total_of(0), total_of(1)
            sigma = 1.0 / (1.0 + jnp.exp(-gate))
            live = gate * sigma
            hidden = live * upward
            slope = upward * sigma * (1.0 + gate * (1.0 - sigma))
            if total % n:
                mine = first_chunk + c >= g_me * n
                hidden, live, slope = (jnp.where(mine, v, 0.0) for v in (hidden, live, slope))
            coef[c, 0] = slope
            coef[c, 1] = live
            act[c, k_me, 0] = hidden.astype(BF)
        else:
            back = total_of(2)
            act[c, k_me, 1] = (back * coef[c, 0]).astype(BF)
            act[c, k_me, 2] = (back * coef[c, 1]).astype(BF)

    def ja(t):
        return pl.ds(0, 1) if t == 0 else pl.ds(1, 2)

    def act_copy(t, c):
        return rcopy(act.at[c, k_me, ja(t)], act.at[c, k_me, ja(t)], a_send.at[t, c], a_recv.at[t, c], partner)

    def act_wait(t, c):
        dst = act.at[c, 1 - k_me, ja(t)]
        rcopy(dst, dst, a_send.at[t, c], a_recv.at[t, c], partner).wait_recv()

    def lhs(c, j):
        return jnp.concatenate([act[c, 0, j].astype(F32), act[c, 1, j].astype(F32)], axis=0).astype(BF)


    def acc_of(q):
        acc = mixed if q < PARTS else grad
        return acc, pl.ds((q % PARTS) * pw, pw)

    def y_stage(q):
        acc, cols = acc_of(q)
        ysend[q] = acc[half:, cols].astype(BF)

    def y_copy(q):
        return rcopy(ysend.at[q], yrecv.at[q], y_send.at[q], y_recv.at[q], across)

    def span(s):
        return nb >> (s + 1)

    def z_base(s):
        return nb - (nb >> s)

    def z_copy(q, s):
        blk = pl.ds(z_base(s), span(s))
        return rcopy(zsend.at[q, blk], zrecv.at[q, blk], z_send.at[q, s], z_recv.at[q, s], zpeer(bits[s]))

    def z_stage(q, s):
        acc, cols = acc_of(q)
        if s == 0:
            y_copy(q).wait_recv()
            ysum[q] = acc[:half, cols] + yrecv[q].astype(F32)
        else:
            z_copy(q, s - 1).wait_recv()
            for i in range(span(s - 1)):
                p = i << s
                r = pl.ds(p * rows, rows)
                ysum[q, r, :] = ysum[q, r, :] + zrecv[q, z_base(s - 1) + i].astype(F32)
        if s < steps:
            for i in range(span(s)):
                p = (2 * i + 1) << s
                zsend[q, z_base(s) + i] = ysum[q, p * rows:(p + 1) * rows, :].astype(BF)
        else:
            out[q // PARTS, :, cols] = ysum[q, :rows, :].astype(BF)


    early = min(EARLY, n)
    for c in range(early):
        for cp in load_gu(c):
            cp.start()
    for w in range(2):
        own_copy(w).start()

    barrier = pltpu.get_barrier_semaphore()
    peers = [partner, across] + [zpeer(m) for m in bits] + [xpeer(d) for d in range(1, chips)]
    for where in peers:
        pl.semaphore_signal(barrier, inc=1, device_id=where, device_id_type=MESH)
    pl.semaphore_wait(barrier, len(peers))

    for w in range(2):
        tok_forward(w, 0)
    for c in range(early, n):
        for cp in load_gu(c):
            cp.start()
    for c in range(n):
        load_d(c).start()
    for e in range(1, nb):
        for w in range(2):
            tok_forward(w, e)
    pack(0, mixed, tok)

    def valid(c):
        return jnp.logical_and(c >= 0, c < n)

    def when_valid(c, f):
        pl.when(valid(c))(lambda: f(c))

    two = 2
    groups = pl.cdiv(n, two)

    def members(m):
        return [m * two + i for i in range(two)]

    def each(m, f):
        for c in members(m):
            when_valid(c, f)

    def top(t):
        when_valid(t - 1, lambda c: pair_copy(0, c).start())
        when_valid(t - 4, lambda c: far_start(0, c))

    def bottom(t):
        when_valid(t - 3, lambda c: chip_sum(0, c))

    def keep(c, j, v):
        part[c, 0, j] = v[:half]
        part[c, 1, j] = v[half:]


    def forward(i, _):
        top(i)
        for cp in load_gu(i):
            cp.wait()
        keep(i, 0, jnp.dot(tok[...], wg[i], preferred_element_type=F32))
        keep(i, 1, jnp.dot(tok[...], wu[i], preferred_element_type=F32))
        bottom(i)
        return 0

    lax.fori_loop(0, n, forward, 0)
    pack(1, grad, cot)
    mixed[...] = jnp.zeros_like(mixed)
    grad[...] = jnp.zeros_like(grad)


    def b_top(m):
        each(m - 1, lambda c: pair_copy(1, c).start())
        each(m - 3, lambda c: far_start(1, c))

    def b_bottom(m):
        each(m - 2, lambda c: chip_sum(1, c))

    def grouped(f):
        lax.fori_loop(0, n // two, lambda m, _: f(m, members(m)) or 0, 0)
        if n % two:
            m = jnp.int32(n // two)
            f(m, [c for c in range((n // two) * two, n)])

    def backward(m, cs):
        top(n + m)
        b_top(m)
        activate(0, m)
        for c in cs:
            load_d(c).wait()
        for c in cs:
            keep(c, 2, lax.dot_general(cot[...], wd[c], NT, preferred_element_type=F32))
        act_copy(0, m).start()
        bottom(n + m)
        b_bottom(m)

    grouped(backward)

    def mix(m, cs):
        b_top(groups + m)
        when_valid(groups + m, lambda c: activate(0, c))
        for c in cs:
            act_wait(0, c)
        acc = 0.0
        for c in cs:
            acc = acc + jnp.dot(lhs(c, 0), wd[c], preferred_element_type=F32)
        mixed[...] += acc
        when_valid(groups + m, lambda c: act_copy(0, c).start())
        b_bottom(groups + m)

    grouped(mix)

    ahead = 2
    for g in range(ahead):
        each(jnp.int32(g), lambda c: activate(1, c))
    for q in range(PARTS):
        y_stage(q)
    for g in range(ahead):
        each(jnp.int32(g), lambda c: act_copy(1, c).start())

    def add_grad(lo, hi, cs):
        acc = 0.0
        for c in cs:
            acc = acc + lax.dot_general(lhs(c, 1), wg[c, lo:hi, :], NT, preferred_element_type=F32)
            acc = acc + lax.dot_general(lhs(c, 2), wu[c, lo:hi, :], NT, preferred_element_type=F32)
        grad[:, lo:hi] += acc

    dh = depth // 2

    def grad_a(m, cs):
        @pl.when(m == 0)
        def _():
            for q in range(PARTS):
                y_copy(q).start()

        each(m + ahead, lambda c: activate(1, c))
        for c in cs:
            act_wait(1, c)
        add_grad(0, dh, cs)
        each(m + ahead, lambda c: act_copy(1, c).start())

    grouped(grad_a)

    mh, gh = range(PARTS), range(PARTS, PARTS + PARTS // 2)
    gl = range(PARTS + PARTS // 2, 2 * PARTS)
    for q in gh:
        y_stage(q)
    for q in mh:
        z_stage(q, 0)

    def grad_b(m, cs):
        @pl.when(m == 0)
        def _():
            for q in mh:
                z_copy(q, 0).start()
            for q in gh:
                y_copy(q).start()

        add_grad(dh, depth, cs)

    grouped(grad_b)

    for q in gl:
        y_stage(q)
    for q in mh:
        z_stage(q, 1)
    for q in gl:
        y_copy(q).start()
    for q in gh:
        z_stage(q, 0)
    def z_start(q, s):
        if s < steps:
            z_copy(q, s).start()

    for q in mh:
        z_start(q, 1)
    for q in gh:
        z_start(q, 0)
    for q in gl:
        z_stage(q, 0)
    for q in gl:
        z_start(q, 0)
    for s in range(2, steps + 1):
        for q in mh:
            z_stage(q, s)
        for q in mh:
            z_start(q, s)
    for s in range(1, steps + 1):
        for q in (*gh, *gl):
            z_stage(q, s)
        for q in (*gh, *gl):
            z_start(q, s)


    for w in range(2):
        for e in range(2 * nb):
            for m in later(e):
                tok_copy(w, e, m).wait_send()

    def drain(c, _):
        for t in range(2):
            pair_copy(t, c).wait_send()
            for d in range(1, chips):
                far_copy(t, c, d).wait_send()
            act_copy(t, c).wait_send()
        return 0

    lax.fori_loop(0, n, drain, 0)
    for q in range(2 * PARTS):
        y_copy(q).wait_send()
        for s in range(steps):
            z_copy(q, s).wait_send()


def per_device(ng, nb, nu, tokens, cotangent, gate_weight, up_weight, down_weight):
    rows, depth = tokens.shape
    width = gate_weight.shape[1]
    fc = next(w for w in (256, 128) if width % w == 0)
    total = width // fc
    n = pl.cdiv(total, ng)
    chips = nu // 2
    assert ng == 2 and nb & (nb - 1) == 0 and nb > 1 and nu % 2 == 0 and chips > 1
    assert n >= 7 and depth % (128 * PARTS) == 0 and (rows * nb) % 8 == 0
    half = rows * nb
    t = 2 * half
    pw = depth // PARTS
    steps = nb.bit_length() - 1
    dma = pltpu.SemaphoreType.DMA
    vm = pltpu.VMEM
    both = pl.pallas_call(
        functools.partial(kernel, nb, nu, n, total, fc),
        out_shape=jax.ShapeDtypeStruct((2, rows, depth), BF),
        in_specs=[pl.BlockSpec(memory_space=pl.ANY)] * 5,
        out_specs=pl.BlockSpec(memory_space=pltpu.VMEM),
        scratch_shapes=[
            vm((n, depth, fc), BF), vm((n, depth, fc), BF), vm((n, fc, depth), BF),
            vm((2, 2 * nb, rows, depth), BF), vm((t, depth), BF), vm((t, depth), BF),
            vm((n, 2, 3, half, fc), F32), vm((n, 3, half, fc), F32), vm((n, 3, half, fc), BF),
            vm((n, chips - 1, 3, half, fc), BF), vm((n, 2, half, fc), F32), vm((n, 2, 3, half, fc), BF),
            vm((t, depth), F32), vm((t, depth), F32),
            vm((2 * PARTS, half, pw), BF), vm((2 * PARTS, half, pw), BF), vm((2 * PARTS, half, pw), F32),
            vm((2 * PARTS, nb - 1, rows, pw), BF), vm((2 * PARTS, nb - 1, rows, pw), BF),
            dma((n,)), dma((n,)), dma((n,)), dma((2,)),
            dma((2, 2 * nb, steps + 1)), dma((2, 2 * nb)),
            dma((2, n)), dma((2, n)),
            dma((2, n, chips - 1)), dma((2, n, chips - 1)),
            dma((2, n)), dma((2, n)),
            dma((2 * PARTS,)), dma((2 * PARTS,)),
            dma((2 * PARTS, steps)), dma((2 * PARTS, steps)),
        ],
        compiler_params=pltpu.CompilerParams(
            collective_id=0, has_side_effects=True, vmem_limit_bytes=67043328),
    )(tokens, cotangent, gate_weight, up_weight, down_weight)
    return both[0], both[1]


def solution(mesh):
    return jax.shard_map(
        functools.partial(per_device, mesh.shape["grp"], mesh.shape["blk"], mesh.shape["bulk"]),
        mesh=mesh,
        in_specs=(
            P(("grp", "blk"), "bulk"),
            P(("grp", "blk"), "bulk"),
            P("bulk", "blk"),
            P("bulk", "blk"),
            P("blk", "bulk"),
        ),
        out_specs=(P(("grp", "blk"), "bulk"), P(("grp", "blk"), "bulk")),
        check_vma=False,
    )
```

```python
import functools

import jax
import jax.numpy as jnp
from jax import lax
from jax.experimental import pallas as pl
from jax.experimental.pallas import tpu as pltpu
from jax.sharding import PartitionSpec as P

MESH = pl.DeviceIdType.MESH
BF = jnp.bfloat16
F32 = jnp.float32
NT = (((1,), (1,)), ((), ()))
EARLY = 4
PARTS = 4


def flip(i, m):
    return i + m - 2 * m * ((i // m) % 2)


def kernel(nb, nu, n, total, fc, tok_in, cot_in, wg_hbm, wu_hbm, wd_hbm, out,
           wgu, wd, got, tok, cot, part, pair, chip, far, coef, act,
           mixed, grad, ysend, yrecv, ysum, zsend, zrecv,
           gu_sem, d_sem, own_sem, tk_send, tk_recv, p_send, p_recv,
           f_send, f_recv, a_send, a_recv, y_send, y_recv, z_send, z_recv):
    g_me = lax.axis_index("grp")
    b_me = lax.axis_index("blk")
    u_me = lax.axis_index("bulk")
    x_me, k_me = u_me // 2, u_me % 2
    chips = nu // 2
    rows, depth = tok_in.shape
    half = nb * rows
    pw = depth // PARTS
    two, four = 2, 4
    groups = pl.cdiv(n, two)
    steps = nb.bit_length() - 1
    bits = [1 << s for s in range(steps)]
    first_chunk = jnp.minimum(g_me * n, total - n)
    partner = {"bulk": x_me * 2 + (1 - k_me)}
    across = {"grp": 1 - g_me}

    def zpeer(m):
        return {"blk": flip(b_me, m)}

    def xpeer(d):
        return {"bulk": ((x_me + d) % chips) * 2 + k_me}

    def rcopy(src, dst, ss, rs, where):
        return pltpu.make_async_remote_copy(
            src_ref=src, dst_ref=dst, send_sem=ss, recv_sem=rs, device_id=where, device_id_type=MESH)


    def load_gu(c):
        cols = pl.ds(pl.multiple_of((first_chunk + c) * fc, fc), fc)
        return (pltpu.make_async_copy(wg_hbm.at[:, cols], wgu.at[c, 0], gu_sem.at[c]),
                pltpu.make_async_copy(wu_hbm.at[:, cols], wgu.at[c, 1], gu_sem.at[c]))

    def wait_gu(c):
        pltpu.make_async_copy(wgu.at[c], wgu.at[c], gu_sem.at[c]).wait()

    def load_d(m, c, cnt):
        src = pl.ds(pl.multiple_of((first_chunk + c) * fc, fc), cnt * fc)
        dst = pl.ds(pl.multiple_of(c * fc, fc), cnt * fc)
        return pltpu.make_async_copy(wd_hbm.at[src, :], wd.at[dst, :], d_sem.at[m])

    def wd_of(c):
        return wd[pl.ds(pl.multiple_of(c * fc, fc), fc), :]


    dims = bits[::-1] + [nb]

    def across_dim(m):
        return across if m == nb else zpeer(m)

    def tok_copy(w, e, m):
        return rcopy(got.at[w, e], got.at[w, e + m], tk_send.at[w], tk_recv.at[w, e + m], across_dim(m))

    def later(e):
        last = max([i for i, m in enumerate(dims) if (e // m) % 2], default=-1)
        return dims[last + 1:]

    def tok_forward(w, e):
        if e:
            rcopy(got.at[w, e], got.at[w, e], tk_send.at[w], tk_recv.at[w, e], across).wait_recv()
        for m in later(e):
            tok_copy(w, e, m).start()

    def own_copy(w):
        return pltpu.make_async_copy((tok_in, cot_in)[w], got.at[w, 0], own_sem.at[w])

    def pack(w, scratch, dst):
        for e in range(2 * nb):
            if e >= nb:
                tok_forward(w, e)
            scratch[e * rows:(e + 1) * rows, :] = got[w, e].astype(F32)
        dst[...] = scratch[...].astype(BF)


    def js(t):
        return pl.ds(0, 2) if t == 0 else pl.ds(2, 1)

    def rows_of(t, m, cnt):
        return pl.ds(m if t == 0 else m * two, cnt)

    def pair_copy(t, m, cnt):
        r = rows_of(t, m, cnt)
        return rcopy(part.at[r, 1 - k_me, js(t)], pair.at[r, js(t)], p_send.at[t], p_recv.at[t, m], partner)

    def chip_sum(t, m, cnt):
        pair_copy(t, m, cnt).wait_recv()
        for i in range(cnt):
            c = m if t == 0 else m * two + i
            for j in ((0, 1), (2,))[t]:
                chip[c, j] = (part[c, k_me, j] + pair[c, j]).astype(BF)

    def far_copy(t, m, cnt, d):
        r = rows_of(t, m, cnt)
        return rcopy(chip.at[r, js(t)], far.at[d - 1, r, js(t)], f_send.at[t, d - 1], f_recv.at[t, m, d - 1],
                     xpeer(d))

    def far_start(t, m, cnt):
        for d in range(1, chips):
            far_copy(t, m, cnt, d).start()

    def activate(t, m, cnt):
        for d in range(1, chips):
            far_copy(t, m, cnt, d).wait_recv()
        for i in range(cnt):
            values(t, m if t == 0 else m * two + i)

    def values(t, c):
        def total_of(j):
            s = part[c, k_me, j] + pair[c, j]
            for d in range(1, chips):
                s = s + far[d - 1, c, j].astype(F32)
            return s

        if t == 0:
            gate, upward = total_of(0), total_of(1)
            sigma = 1.0 / (1.0 + jnp.exp(-gate))
            live = gate * sigma
            hidden = live * upward
            slope = upward * sigma * (1.0 + gate * (1.0 - sigma))
            if total % n:
                mine = first_chunk + c >= g_me * n
                hidden, live, slope = (jnp.where(mine, v, 0.0) for v in (hidden, live, slope))
            coef[c, 0] = slope
            coef[c, 1] = live
            act[c, k_me, 0] = hidden.astype(BF)
        else:
            back = total_of(2)
            act[c, k_me, 1] = (back * coef[c, 0]).astype(BF)
            act[c, k_me, 2] = (back * coef[c, 1]).astype(BF)

    def ja(t):
        return pl.ds(0, 1) if t == 0 else pl.ds(1, 2)

    def act_copy(t, m, cnt):
        r = rows_of(t, m, cnt)
        ref = act.at[r, k_me, ja(t)]
        return rcopy(ref, ref, a_send.at[t], a_recv.at[t, m], partner)

    def act_wait(t, m, cnt):
        ref = act.at[rows_of(t, m, cnt), 1 - k_me, ja(t)]
        rcopy(ref, ref, a_send.at[t], a_recv.at[t, m], partner).wait_recv()

    def lhs(c, j):
        return jnp.concatenate([act[c, 0, j].astype(F32), act[c, 1, j].astype(F32)], axis=0).astype(BF)


    outs = [(0, PARTS), (PARTS, 2), (PARTS + 2, 1), (PARTS + 3, 1)]

    def acc_of(q):
        acc = mixed if q < PARTS else grad
        return acc, pl.ds((q % PARTS) * pw, pw)

    def run(o):
        return range(outs[o][0], sum(outs[o]))

    def y_stage(o):
        for q in run(o):
            acc, cols = acc_of(q)
            ysend[q] = acc[half:, cols].astype(BF)

    def y_copy(o):
        qs = pl.ds(*outs[o])
        return rcopy(ysend.at[qs], yrecv.at[qs], y_send.at[0], y_recv.at[o], across)

    def span(s):
        return nb >> (s + 1)

    def z_base(s):
        return nb - (nb >> s)

    def z_copy(o, s):
        at = (pl.ds(*outs[o]), pl.ds(z_base(s), span(s)))
        return rcopy(zsend.at[at], zrecv.at[at], z_send.at[s], z_recv.at[o, s], zpeer(bits[s]))

    def z_stage(o, s):
        (y_copy(o) if s == 0 else z_copy(o, s - 1)).wait_recv()
        for q in run(o):
            acc, cols = acc_of(q)
            if s == 0:
                ysum[q] = acc[:half, cols] + yrecv[q].astype(F32)
            else:
                for i in range(span(s - 1)):
                    p = i << s
                    r = pl.ds(p * rows, rows)
                    ysum[q, r, :] = ysum[q, r, :] + zrecv[q, z_base(s - 1) + i].astype(F32)
            if s < steps:
                for i in range(span(s)):
                    p = (2 * i + 1) << s
                    zsend[q, z_base(s) + i] = ysum[q, p * rows:(p + 1) * rows, :].astype(BF)
            else:
                out[q // PARTS, :, cols] = ysum[q, :rows, :].astype(BF)

    def z_start(o, s):
        if s < steps:
            z_copy(o, s).start()

    def z_step(o, s):
        if s <= steps:
            z_stage(o, s)
            z_start(o, s)


    def valid(c):
        return jnp.logical_and(c >= 0, c < n)

    def chunk(c, f):
        pl.when(valid(c))(lambda: f(c, 1))

    def group(m, f):
        pl.when(jnp.logical_and(m >= 0, m < n // two))(lambda: f(m, two))
        if n % two:
            pl.when(m == n // two)(lambda: f(n // two, n % two))

    def grouped(size, f):
        lax.fori_loop(0, n // size, lambda m, _: f(m, [m * size + i for i in range(size)]) or 0, 0)
        if n % size:
            f(jnp.int32(n // size), list(range(n - n % size, n)))

    def at(m, size, k, f):
        pl.when(m == min(k, pl.cdiv(n, size) - 1))(f)


    early = min(EARLY, n)
    own_copy(0).start()
    own_copy(1).start()
    for c in range(early):
        for cp in load_gu(c):
            cp.start()

    barrier = pltpu.get_barrier_semaphore()
    peers = [partner, across] + [zpeer(m) for m in bits] + [xpeer(d) for d in range(1, chips)]
    for where in peers:
        pl.semaphore_signal(barrier, inc=1, device_id=where, device_id_type=MESH)
    own_copy(0).wait()
    own_copy(1).wait()
    pl.semaphore_wait(barrier, len(peers))

    tok_forward(0, 0)
    for c in range(early, n):
        for cp in load_gu(c):
            cp.start()
    for m in range(groups):
        load_d(m, m * two, min(two, n - m * two)).start()
    for e in range(1, nb):
        tok_forward(0, e)
    tok_forward(1, 0)
    pack(0, mixed, tok)

    def top(t):
        chunk(t - 1, lambda c, i: pair_copy(0, c, i).start())
        chunk(t - 4, lambda c, i: far_start(0, c, i))

    def bottom(t):
        chunk(t - 3, lambda c, i: chip_sum(0, c, i))

    def keep(c, j, v):
        part[c, 0, j] = v[:half]
        part[c, 1, j] = v[half:]


    def forward(i, _):
        top(i)
        for e in range(1, nb):
            at(i, 1, 4 + (6 * (e - 1)) // (nb - 1), lambda e=e: tok_forward(1, e))
        wait_gu(i)
        keep(i, 0, jnp.dot(tok[...], wgu[i, 0], preferred_element_type=F32))
        keep(i, 1, jnp.dot(tok[...], wgu[i, 1], preferred_element_type=F32))
        bottom(i)
        return 0

    lax.fori_loop(0, n, forward, 0)
    pack(1, grad, cot)
    mixed[...] = jnp.zeros_like(mixed)
    grad[...] = jnp.zeros_like(grad)


    def b_top(m):
        group(m - 1, lambda g, i: pair_copy(1, g, i).start())
        group(m - 3, lambda g, i: far_start(1, g, i))

    def b_bottom(m):
        group(m - 2, lambda g, i: chip_sum(1, g, i))

    def backward(m, cs):
        top(n + m)
        b_top(m)
        activate(0, m, 1)
        load_d(m, cs[0], len(cs)).wait()
        for c in cs:
            keep(c, 2, lax.dot_general(cot[...], wd_of(c), NT, preferred_element_type=F32))
        act_copy(0, m, 1).start()
        bottom(n + m)
        b_bottom(m)

    grouped(two, backward)

    def mix(m, cs):
        b_top(groups + m)
        chunk(groups + m, lambda c, i: activate(0, c, i))
        for c in cs:
            act_wait(0, c, 1)
        acc = 0.0
        for c in cs:
            acc = acc + jnp.dot(lhs(c, 0), wd_of(c), preferred_element_type=F32)
        mixed[...] += acc
        chunk(groups + m, lambda c, i: act_copy(0, c, i).start())
        b_bottom(groups + m)

    grouped(two, mix)

    def add_grad(lo, hi, cs):
        acc = 0.0
        for c in cs:
            acc = acc + lax.dot_general(lhs(c, 1), wgu[c, 0, lo:hi, :], NT, preferred_element_type=F32)
            acc = acc + lax.dot_general(lhs(c, 2), wgu[c, 1, lo:hi, :], NT, preferred_element_type=F32)
        grad[:, lo:hi] += acc

    ahead = 2
    for g in range(ahead):
        activate(1, g, two)
    y_stage(0)
    for g in range(ahead):
        act_copy(1, g, two).start()

    def grad_a(m, cs):
        at(m, two, 0, lambda: y_copy(0).start())
        at(m, two, 5, lambda: z_stage(0, 0))
        at(m, two, 6, lambda: z_start(0, 0))
        group(m + ahead, lambda g, i: activate(1, g, i))
        act_wait(1, m, len(cs))
        add_grad(0, 2 * pw, cs)
        group(m + ahead, lambda g, i: act_copy(1, g, i).start())

    grouped(two, grad_a)
    y_stage(1)

    def grad_b(m, cs):
        at(m, four, 0, lambda: y_copy(1).start())
        at(m, four, 2, lambda: z_stage(0, 1))
        at(m, four, 3, lambda: z_start(0, 1))
        add_grad(2 * pw, 3 * pw, cs)

    grouped(four, grad_b)
    y_stage(2)

    def grad_c(m, cs):
        at(m, four, 0, lambda: y_copy(2).start())
        at(m, four, 1, lambda: z_stage(1, 0))
        at(m, four, 2, lambda: z_start(1, 0))
        add_grad(3 * pw, depth, cs)

    grouped(four, grad_c)
    y_stage(3)
    y_copy(3).start()
    z_step(2, 0)
    z_step(1, 1)
    z_step(0, 2)
    z_step(2, 1)
    z_step(3, 0)
    z_step(1, 2)
    z_step(3, 1)
    z_step(2, 2)
    z_step(3, 2)
    for s in range(3, steps + 1):
        for o in range(len(outs)):
            z_step(o, s)


    def left(ref, sem):
        rcopy(ref, ref, sem, sem, across).wait_send()

    for w in range(2):
        left(got.at[w, pl.ds(1, 2 * nb - 1)], tk_send.at[w])
    for t in range(2):
        left(part.at[:, 0, js(t)], p_send.at[t])
        for d in range(1, chips):
            left(chip.at[:, js(t)], f_send.at[t, d - 1])
        left(act.at[:, 0, ja(t)], a_send.at[t])
    left(ysend, y_send.at[0])
    for s in range(steps):
        left(zsend.at[:, pl.ds(z_base(s), span(s))], z_send.at[s])


def per_device(ng, nb, nu, tokens, cotangent, gate_weight, up_weight, down_weight):
    rows, depth = tokens.shape
    width = gate_weight.shape[1]
    fc = next(w for w in (256, 128) if width % w == 0)
    total = width // fc
    n = pl.cdiv(total, ng)
    chips = nu // 2
    assert ng == 2 and nb & (nb - 1) == 0 and nb > 1 and nu % 2 == 0 and chips > 1
    assert n >= 7 and depth % (128 * PARTS) == 0 and (rows * nb) % 8 == 0
    half = rows * nb
    t = 2 * half
    pw = depth // PARTS
    steps = nb.bit_length() - 1
    dma = pltpu.SemaphoreType.DMA
    vm = pltpu.VMEM
    both = pl.pallas_call(
        functools.partial(kernel, nb, nu, n, total, fc),
        out_shape=vm((2, rows, depth), BF),
        in_specs=[pl.BlockSpec(memory_space=pl.ANY)] * 5,
        out_specs=pl.BlockSpec(memory_space=pltpu.VMEM),
        scratch_shapes=[
            vm((n, 2, depth, fc), BF), vm((n * fc, depth), BF),
            vm((2, 2 * nb, rows, depth), BF), vm((t, depth), BF), vm((t, depth), BF),
            vm((n, 2, 3, half, fc), F32), vm((n, 3, half, fc), F32), vm((n, 3, half, fc), BF),
            vm((chips - 1, n, 3, half, fc), BF), vm((n, 2, half, fc), F32), vm((n, 2, 3, half, fc), BF),
            vm((t, depth), F32), vm((t, depth), F32),
            vm((2 * PARTS, half, pw), BF), vm((2 * PARTS, half, pw), BF), vm((2 * PARTS, half, pw), F32),
            vm((2 * PARTS, nb - 1, rows, pw), BF), vm((2 * PARTS, nb - 1, rows, pw), BF),
            dma((n,)), dma((pl.cdiv(n, 2),)), dma((2,)), dma((2,)), dma((2, 2 * nb)),
            dma((2,)), dma((2, n)), dma((2, chips - 1)), dma((2, n, chips - 1)), dma((2,)), dma((2, n)),
            dma((1,)), dma((PARTS,)), dma((steps,)), dma((PARTS, steps)),
        ],
        compiler_params=pltpu.CompilerParams(
            collective_id=0, has_side_effects=True, vmem_limit_bytes=67043328 - 4 * depth * pl.cdiv(rows, 16) * 16),
    )(tokens, cotangent, gate_weight, up_weight, down_weight)
    return both[0], both[1]


def solution(mesh):
    return jax.shard_map(
        functools.partial(per_device, mesh.shape["grp"], mesh.shape["blk"], mesh.shape["bulk"]),
        mesh=mesh,
        in_specs=(
            P(("grp", "blk"), "bulk"),
            P(("grp", "blk"), "bulk"),
            P("bulk", "blk"),
            P("bulk", "blk"),
            P("blk", "bulk"),
        ),
        out_specs=(P(("grp", "blk"), "bulk"), P(("grp", "blk"), "bulk")),
        check_vma=False,
    )
```

```python
import functools

import jax
import jax.numpy as jnp
from jax import lax
from jax.experimental import pallas as pl
from jax.experimental.pallas import tpu as pltpu
from jax.sharding import PartitionSpec as P

MESH = pl.DeviceIdType.MESH
BF = jnp.bfloat16
F32 = jnp.float32
NT = (((1,), (1,)), ((), ()))
PARTS = 4


def flip(i, m):
    return i + m - 2 * m * ((i // m) % 2)


def kernel(nb, nu, n, total, fc, tok_in, cot_in, wg_hbm, wu_hbm, wd_hbm, out,
           wgu, wd, own, folded, got, tok, cot, part, pair, chip, far, coef, act,
           mixed, grad, ysend, yrecv, ysum, zsend, zrecv,
           gu_sem, d_sem, own_sem, tk_send, tk_recv, p_send, p_recv,
           f_send, f_recv, a_send, a_recv, y_send, y_recv, z_send, z_recv):
    g_me = lax.axis_index("grp")
    b_me = lax.axis_index("blk")
    u_me = lax.axis_index("bulk")
    x_me, k_me = u_me // 2, u_me % 2
    chips = nu // 2
    rows, depth = tok_in.shape
    half = nb * rows
    pw = depth // PARTS
    two, four = 2, 4
    groups = pl.cdiv(n, two)
    steps = nb.bit_length() - 1
    bits = [1 << s for s in range(steps)]
    first_chunk = jnp.minimum(g_me * n, total - n)
    partner = {"bulk": x_me * 2 + (1 - k_me)}
    across = {"grp": 1 - g_me}

    def zpeer(m):
        return {"blk": flip(b_me, m)}

    def xpeer(d):
        return {"bulk": ((x_me + d) % chips) * 2 + k_me}

    def rcopy(src, dst, ss, rs, where):
        return pltpu.make_async_remote_copy(
            src_ref=src, dst_ref=dst, send_sem=ss, recv_sem=rs, device_id=where, device_id_type=MESH)


    def load_gu(c):
        cols = pl.ds(pl.multiple_of((first_chunk + c) * fc, fc), fc)
        return (pltpu.make_async_copy(wg_hbm.at[:, cols], wgu.at[c, 0], gu_sem.at[c]),
                pltpu.make_async_copy(wu_hbm.at[:, cols], wgu.at[c, 1], gu_sem.at[c]))

    def wait_gu(c):
        pltpu.make_async_copy(wgu.at[c], wgu.at[c], gu_sem.at[c]).wait()

    def load_d(m, c, cnt):
        src = pl.ds(pl.multiple_of((first_chunk + c) * fc, fc), cnt * fc)
        dst = pl.ds(pl.multiple_of(c * fc, fc), cnt * fc)
        return pltpu.make_async_copy(wd_hbm.at[src, :], wd.at[dst, :], d_sem.at[m])

    def wd_of(c):
        return wd[pl.ds(pl.multiple_of(c * fc, fc), fc), :]


    dims = bits[::-1] + [nb]
    fold, wide = got.shape[3] // rows, got.shape[4]

    def across_dim(m):
        return across if m == nb else zpeer(m)

    def tok_ref(w, e, h):
        return got.at[w, e, h]

    def tok_copy(w, e, m, h):
        return rcopy(tok_ref(w, e, h), tok_ref(w, e + m, h), tk_send.at[w], tk_recv.at[w, e + m, h], across_dim(m))

    def tok_wait(w, e, h):
        rcopy(tok_ref(w, e, h), tok_ref(w, e, h), tk_send.at[w], tk_recv.at[w, e, h], across).wait_recv()

    def later(e):
        last = max([i for i, m in enumerate(dims) if (e // m) % 2], default=-1)
        return dims[last + 1:]

    def tok_forward(w, e):
        if e == 0:
            for m in later(e):
                for h in range(2):
                    tok_copy(w, e, m, h).start()
        else:
            for h in range(2):
                tok_wait(w, e, h)
                for m in later(e):
                    tok_copy(w, e, m, h).start()

    def own_copy(w):
        return pltpu.make_async_copy((tok_in, cot_in)[w], own.at[w], own_sem.at[w])

    def place(h, j):
        lo = (h * fold + j) * wide
        return slice(lo, lo + wide)

    def fold_own(w):
        own_copy(w).wait()
        for h in range(2):
            for j in range(fold):
                folded[w, h, j * rows:(j + 1) * rows, :] = own[w, :, place(h, j)].astype(F32)
        got[w, 0] = folded[w].astype(BF)

    def pack(w, scratch, dst):
        for e in range(2 * nb):
            for h in range(2):
                if e >= nb:
                    tok_wait(w, e, h)
                for j in range(fold):
                    scratch[e * rows:(e + 1) * rows, place(h, j)] = (
                        got[w, e, h, j * rows:(j + 1) * rows, :].astype(F32))
        dst[...] = scratch[...].astype(BF)


    def js(t):
        return pl.ds(0, 2) if t == 0 else pl.ds(2, 1)

    def rows_of(t, m, cnt):
        return pl.ds(m if t == 0 else m * two, cnt)

    def pair_copy(t, m, cnt):
        r = rows_of(t, m, cnt)
        return rcopy(part.at[r, 1 - k_me, js(t)], pair.at[r, js(t)], p_send.at[t], p_recv.at[t, m], partner)

    def chip_sum(t, m, cnt):
        pair_copy(t, m, cnt).wait_recv()
        for i in range(cnt):
            c = m if t == 0 else m * two + i
            for j in ((0, 1), (2,))[t]:
                chip[c, j] = (part[c, k_me, j] + pair[c, j]).astype(BF)

    def far_copy(t, m, cnt, d):
        r = rows_of(t, m, cnt)
        return rcopy(chip.at[r, js(t)], far.at[d - 1, r, js(t)], f_send.at[t, d - 1], f_recv.at[t, m, d - 1],
                     xpeer(d))

    def far_start(t, m, cnt):
        for d in range(1, chips):
            far_copy(t, m, cnt, d).start()

    def activate(t, m, cnt):
        for d in range(1, chips):
            far_copy(t, m, cnt, d).wait_recv()
        for i in range(cnt):
            values(t, m if t == 0 else m * two + i)

    def values(t, c):
        def total_of(j):
            s = part[c, k_me, j] + pair[c, j]
            for d in range(1, chips):
                s = s + far[d - 1, c, j].astype(F32)
            return s

        if t == 0:
            gate, upward = total_of(0), total_of(1)
            sigma = 1.0 / (1.0 + jnp.exp(-gate))
            live = gate * sigma
            hidden = live * upward
            slope = upward * sigma * (1.0 + gate * (1.0 - sigma))
            if total % n:
                mine = first_chunk + c >= g_me * n
                hidden, live, slope = (jnp.where(mine, v, 0.0) for v in (hidden, live, slope))
            coef[c, 0] = slope
            coef[c, 1] = live
            act[c, k_me, 0] = hidden.astype(BF)
        else:
            back = total_of(2)
            act[c, k_me, 1] = (back * coef[c, 0]).astype(BF)
            act[c, k_me, 2] = (back * coef[c, 1]).astype(BF)

    def ja(t):
        return pl.ds(0, 1) if t == 0 else pl.ds(1, 2)

    def act_copy(t, m, cnt):
        r = rows_of(t, m, cnt)
        ref = act.at[r, k_me, ja(t)]
        return rcopy(ref, ref, a_send.at[t], a_recv.at[t, m], partner)

    def act_wait(t, m, cnt):
        ref = act.at[rows_of(t, m, cnt), 1 - k_me, ja(t)]
        rcopy(ref, ref, a_send.at[t], a_recv.at[t, m], partner).wait_recv()

    def lhs(c, j):
        return jnp.concatenate([act[c, 0, j].astype(F32), act[c, 1, j].astype(F32)], axis=0).astype(BF)


    outs = [(0, PARTS), (PARTS, 2), (PARTS + 2, 1), (PARTS + 3, 1)]

    def acc_of(q):
        acc = mixed if q < PARTS else grad
        return acc, pl.ds((q % PARTS) * pw, pw)

    def run(o):
        return range(outs[o][0], sum(outs[o]))

    def y_stage(o):
        for q in run(o):
            acc, cols = acc_of(q)
            ysend[q] = acc[half:, cols].astype(BF)

    def y_copy(o):
        qs = pl.ds(*outs[o])
        return rcopy(ysend.at[qs], yrecv.at[qs], y_send.at[0], y_recv.at[o], across)

    def span(s):
        return nb >> (s + 1)

    def z_base(s):
        return nb - (nb >> s)

    def z_copy(o, s):
        at = (pl.ds(*outs[o]), pl.ds(z_base(s), span(s)))
        return rcopy(zsend.at[at], zrecv.at[at], z_send.at[s], z_recv.at[o, s], zpeer(bits[s]))

    def z_stage(o, s):
        (y_copy(o) if s == 0 else z_copy(o, s - 1)).wait_recv()
        for q in run(o):
            acc, cols = acc_of(q)
            if s == 0:
                ysum[q] = acc[:half, cols] + yrecv[q].astype(F32)
            else:
                for i in range(span(s - 1)):
                    p = i << s
                    r = pl.ds(p * rows, rows)
                    ysum[q, r, :] = ysum[q, r, :] + zrecv[q, z_base(s - 1) + i].astype(F32)
            if s < steps:
                for i in range(span(s)):
                    p = (2 * i + 1) << s
                    zsend[q, z_base(s) + i] = ysum[q, p * rows:(p + 1) * rows, :].astype(BF)
            else:
                out[q // PARTS, :, cols] = ysum[q, :rows, :].astype(BF)

    def z_start(o, s):
        if s < steps:
            z_copy(o, s).start()

    def z_step(o, s):
        if s <= steps:
            z_stage(o, s)
            z_start(o, s)


    def valid(c):
        return jnp.logical_and(c >= 0, c < n)

    def chunk(c, f):
        pl.when(valid(c))(lambda: f(c, 1))

    def group(m, f):
        pl.when(jnp.logical_and(m >= 0, m < n // two))(lambda: f(m, two))
        if n % two:
            pl.when(m == n // two)(lambda: f(n // two, n % two))

    def grouped(size, f):
        lax.fori_loop(0, n // size, lambda m, _: f(m, [m * size + i for i in range(size)]) or 0, 0)
        if n % size:
            f(jnp.int32(n // size), list(range(n - n % size, n)))

    def at(m, size, k, f):
        pl.when(m == min(k, pl.cdiv(n, size) - 1))(f)


    barrier = pltpu.get_barrier_semaphore()
    peers = [partner, across] + [zpeer(m) for m in bits] + [xpeer(d) for d in range(1, chips)]
    for where in peers:
        pl.semaphore_signal(barrier, inc=1, device_id=where, device_id_type=MESH)
    for w in range(2):
        own_copy(w).start()
    for w in range(2):
        fold_own(w)
    for c in range(n):
        for cp in load_gu(c):
            cp.start()
    for m in range(groups):
        load_d(m, m * two, min(two, n - m * two)).start()
    pl.semaphore_wait(barrier, len(peers))

    for w in range(2):
        tok_forward(w, 0)
    for e in range(1, nb):
        tok_forward(0, e)
    for e in range(1, nb - 1):
        tok_forward(1, e)
    pack(0, mixed, tok)

    def top(t):
        chunk(t - 1, lambda c, i: pair_copy(0, c, i).start())
        chunk(t - 4, lambda c, i: far_start(0, c, i))

    def bottom(t):
        chunk(t - 3, lambda c, i: chip_sum(0, c, i))

    def keep(c, j, v):
        part[c, 0, j] = v[:half]
        part[c, 1, j] = v[half:]


    def forward(i, _):
        top(i)
        at(i, 1, 3, lambda: tok_forward(1, nb - 1))
        wait_gu(i)
        keep(i, 0, jnp.dot(tok[...], wgu[i, 0], preferred_element_type=F32))
        keep(i, 1, jnp.dot(tok[...], wgu[i, 1], preferred_element_type=F32))
        bottom(i)
        return 0

    lax.fori_loop(0, n, forward, 0)
    pack(1, grad, cot)
    mixed[...] = jnp.zeros_like(mixed)
    grad[...] = jnp.zeros_like(grad)


    def b_top(m):
        group(m - 1, lambda g, i: pair_copy(1, g, i).start())
        group(m - 3, lambda g, i: far_start(1, g, i))

    def b_bottom(m):
        group(m - 2, lambda g, i: chip_sum(1, g, i))

    def backward(m, cs):
        top(n + m)
        b_top(m)
        activate(0, m, 1)
        load_d(m, cs[0], len(cs)).wait()
        for c in cs:
            keep(c, 2, lax.dot_general(cot[...], wd_of(c), NT, preferred_element_type=F32))
        act_copy(0, m, 1).start()
        bottom(n + m)
        b_bottom(m)

    grouped(two, backward)

    def mix(m, cs):
        b_top(groups + m)
        chunk(groups + m, lambda c, i: activate(0, c, i))
        for c in cs:
            act_wait(0, c, 1)
        acc = 0.0
        for c in cs:
            acc = acc + jnp.dot(lhs(c, 0), wd_of(c), preferred_element_type=F32)
        mixed[...] += acc
        chunk(groups + m, lambda c, i: act_copy(0, c, i).start())
        b_bottom(groups + m)

    grouped(two, mix)

    def add_grad(lo, hi, cs):
        acc = 0.0
        for c in cs:
            acc = acc + lax.dot_general(lhs(c, 1), wgu[c, 0, lo:hi, :], NT, preferred_element_type=F32)
            acc = acc + lax.dot_general(lhs(c, 2), wgu[c, 1, lo:hi, :], NT, preferred_element_type=F32)
        grad[:, lo:hi] += acc

    ahead = 2
    for g in range(ahead):
        activate(1, g, two)
    y_stage(0)
    for g in range(ahead):
        act_copy(1, g, two).start()

    def grad_a(m, cs):
        at(m, two, 0, lambda: y_copy(0).start())
        at(m, two, 5, lambda: z_stage(0, 0))
        at(m, two, 6, lambda: z_start(0, 0))
        group(m + ahead, lambda g, i: activate(1, g, i))
        act_wait(1, m, len(cs))
        add_grad(0, 2 * pw, cs)
        group(m + ahead, lambda g, i: act_copy(1, g, i).start())

    grouped(two, grad_a)
    y_stage(1)

    def grad_b(m, cs):
        at(m, four, 0, lambda: y_copy(1).start())
        at(m, four, 2, lambda: z_stage(0, 1))
        at(m, four, 3, lambda: z_start(0, 1))
        add_grad(2 * pw, 3 * pw, cs)

    grouped(four, grad_b)
    y_stage(2)

    def grad_c(m, cs):
        at(m, four, 0, lambda: y_copy(2).start())
        at(m, four, 1, lambda: z_stage(1, 0))
        at(m, four, 2, lambda: z_start(1, 0))
        add_grad(3 * pw, depth, cs)

    grouped(four, grad_c)
    y_stage(3)
    y_copy(3).start()
    z_step(2, 0)
    z_step(1, 1)
    z_step(0, 2)
    z_step(2, 1)
    z_step(3, 0)
    z_step(1, 2)
    z_step(3, 1)
    z_step(2, 2)
    z_step(3, 2)
    for s in range(3, steps + 1):
        for o in range(len(outs)):
            z_step(o, s)


    def left(ref, sem):
        rcopy(ref, ref, sem, sem, across).wait_send()

    for w in range(2):
        left(got.at[w, pl.ds(1, 2 * nb - 1)], tk_send.at[w])
    for t in range(2):
        left(part.at[:, 0, js(t)], p_send.at[t])
        for d in range(1, chips):
            left(chip.at[:, js(t)], f_send.at[t, d - 1])
        left(act.at[:, 0, ja(t)], a_send.at[t])
    left(ysend, y_send.at[0])
    for s in range(steps):
        left(zsend.at[:, pl.ds(z_base(s), span(s))], z_send.at[s])


def per_device(ng, nb, nu, tokens, cotangent, gate_weight, up_weight, down_weight):
    rows, depth = tokens.shape
    width = gate_weight.shape[1]
    fc = next(w for w in (256, 128) if width % w == 0)
    total = width // fc
    n = pl.cdiv(total, ng)
    chips = nu // 2
    assert ng == 2 and nb & (nb - 1) == 0 and nb > 1 and nu % 2 == 0 and chips > 1
    assert n >= 7 and depth % (128 * PARTS) == 0 and (rows * nb) % 8 == 0
    half = rows * nb
    t = 2 * half
    pw = depth // PARTS
    steps = nb.bit_length() - 1
    fold = next((f for f in (1, 2, 4, 8) if rows * f % 8 == 0 and depth % (256 * f) == 0), 1)
    wide = depth // (2 * fold)
    dma = pltpu.SemaphoreType.DMA
    vm = pltpu.VMEM
    both = pl.pallas_call(
        functools.partial(kernel, nb, nu, n, total, fc),
        out_shape=vm((2, rows, depth), BF),
        in_specs=[pl.BlockSpec(memory_space=pl.ANY)] * 5,
        out_specs=pl.BlockSpec(memory_space=pltpu.VMEM),
        scratch_shapes=[
            vm((n, 2, depth, fc), BF), vm((n * fc, depth), BF),
            vm((2, rows, depth), BF), vm((2, 2, rows * fold, wide), F32),
            vm((2, 2 * nb, 2, rows * fold, wide), BF), vm((t, depth), BF), vm((t, depth), BF),
            vm((n, 2, 3, half, fc), F32), vm((n, 3, half, fc), F32), vm((n, 3, half, fc), BF),
            vm((chips - 1, n, 3, half, fc), BF), vm((n, 2, half, fc), F32), vm((n, 2, 3, half, fc), BF),
            vm((t, depth), F32), vm((t, depth), F32),
            vm((2 * PARTS, half, pw), BF), vm((2 * PARTS, half, pw), BF), vm((2 * PARTS, half, pw), F32),
            vm((2 * PARTS, nb - 1, rows, pw), BF), vm((2 * PARTS, nb - 1, rows, pw), BF),
            dma((n,)), dma((pl.cdiv(n, 2),)), dma((2,)), dma((2,)), dma((2, 2 * nb, 2)),
            dma((2,)), dma((2, n)), dma((2, chips - 1)), dma((2, n, chips - 1)), dma((2,)), dma((2, n)),
            dma((1,)), dma((PARTS,)), dma((steps,)), dma((PARTS, steps)),
        ],
        compiler_params=pltpu.CompilerParams(
            collective_id=0, has_side_effects=True, vmem_limit_bytes=67043328 - 4 * depth * pl.cdiv(rows, 16) * 16),
    )(tokens, cotangent, gate_weight, up_weight, down_weight)
    return both[0], both[1]


def solution(mesh):
    return jax.shard_map(
        functools.partial(per_device, mesh.shape["grp"], mesh.shape["blk"], mesh.shape["bulk"]),
        mesh=mesh,
        in_specs=(
            P(("grp", "blk"), "bulk"),
            P(("grp", "blk"), "bulk"),
            P("bulk", "blk"),
            P("bulk", "blk"),
            P("blk", "bulk"),
        ),
        out_specs=(P(("grp", "blk"), "bulk"), P(("grp", "blk"), "bulk")),
        check_vma=False,
    )
```

```python
import functools

import jax
import jax.numpy as jnp
from jax import lax
from jax.experimental import pallas as pl
from jax.experimental.pallas import tpu as pltpu
from jax.sharding import PartitionSpec as P

MESH = pl.DeviceIdType.MESH
BF = jnp.bfloat16
F32 = jnp.float32
NT = (((1,), (1,)), ((), ()))
PARTS = 4
SIZE = 4


def flip(i, m):
    return i + m - 2 * m * ((i // m) % 2)


def flips(i, bits):
    for s in range(bits.bit_length()):
        if bits >> s & 1:
            i = flip(i, 1 << s)
    return i


def kernel(nb, nu, n, total, fc, tok_in, cot_in, wg_hbm, wu_hbm, wd_hbm, out,
           wgu, wd, own, folded, got, tok, cot, part, pair, chip, far, coef, act,
           mixed, grad, ysend, yrecv, ysum, zflat, zsend, zrecv, lflat, lsend, lrecv,
           gu_sem, d_sem, own_sem, tk_send, tk_recv, p_send, p_recv,
           f_send, f_recv, a_send, a_recv, y_send, y_recv, z_send, z_recv, l_send, l_recv):
    g_me = lax.axis_index("grp")
    b_me = lax.axis_index("blk")
    u_me = lax.axis_index("bulk")
    x_me, k_me = u_me // 2, u_me % 2
    chips = nu // 2
    rows, depth = tok_in.shape
    half = nb * rows
    pw = depth // PARTS
    size = SIZE
    groups = pl.cdiv(n, size)
    steps = nb.bit_length() - 1
    bits = [1 << s for s in range(steps)]
    first_chunk = jnp.minimum(g_me * n, total - n)
    partner = {"bulk": x_me * 2 + (1 - k_me)}
    across = {"grp": 1 - g_me}

    def zpeer(m):
        return {"blk": flip(b_me, m)}

    def xpeer(d):
        return {"bulk": ((x_me + d) % chips) * 2 + k_me}

    def rcopy(src, dst, ss, rs, where):
        return pltpu.make_async_remote_copy(
            src_ref=src, dst_ref=dst, send_sem=ss, recv_sem=rs, device_id=where, device_id_type=MESH)


    def load_gu(c):
        cols = pl.ds(pl.multiple_of((first_chunk + c) * fc, fc), fc)
        return (pltpu.make_async_copy(wg_hbm.at[:, cols], wgu.at[c, 0], gu_sem.at[c]),
                pltpu.make_async_copy(wu_hbm.at[:, cols], wgu.at[c, 1], gu_sem.at[c]))

    def wait_gu(c):
        pltpu.make_async_copy(wgu.at[c], wgu.at[c], gu_sem.at[c]).wait()

    def load_d(m, c, cnt):
        src = pl.ds(pl.multiple_of((first_chunk + c) * fc, fc), cnt * fc)
        dst = pl.ds(pl.multiple_of(c * fc, fc), cnt * fc)
        return pltpu.make_async_copy(wd_hbm.at[src, :], wd.at[dst, :], d_sem.at[m])

    def wd_of(c):
        return wd[pl.ds(pl.multiple_of(c * fc, fc), fc), :]


    dims = bits[::-1] + [nb]
    fold, wide = got.shape[3] // rows, got.shape[4]
    zfold, zwide = zsend.shape[2] // rows, zsend.shape[3]

    def across_dim(m):
        return across if m == nb else zpeer(m)

    def tok_ref(w, e, h):
        return got.at[w, e, h]

    def tok_copy(w, e, m, h):
        return rcopy(tok_ref(w, e, h), tok_ref(w, e + m, h), tk_send.at[w], tk_recv.at[w, e + m, h], across_dim(m))

    def tok_wait(w, e, h):
        rcopy(tok_ref(w, e, h), tok_ref(w, e, h), tk_send.at[w], tk_recv.at[w, e, h], across).wait_recv()

    def later(e):
        last = max([i for i, m in enumerate(dims) if (e // m) % 2], default=-1)
        return dims[last + 1:]

    def tok_forward(w, e):
        if e == 0:
            for m in later(e):
                for h in range(2):
                    tok_copy(w, e, m, h).start()
        else:
            for h in range(2):
                tok_wait(w, e, h)
                for m in later(e):
                    tok_copy(w, e, m, h).start()

    def own_copy(w):
        return pltpu.make_async_copy((tok_in, cot_in)[w], own.at[w], own_sem.at[w])

    def place(h, j):
        lo = (h * fold + j) * wide
        return slice(lo, lo + wide)

    def fold_own(w):
        own_copy(w).wait()
        for h in range(2):
            for j in range(fold):
                folded[w, h, j * rows:(j + 1) * rows, :] = own[w, :, place(h, j)].astype(F32)
        got[w, 0] = folded[w].astype(BF)

    def pack(w, scratch, dst):
        for e in range(2 * nb):
            for h in range(2):
                if e >= nb:
                    tok_wait(w, e, h)
                for j in range(fold):
                    scratch[e * rows:(e + 1) * rows, place(h, j)] = (
                        got[w, e, h, j * rows:(j + 1) * rows, :].astype(F32))
        dst[...] = scratch[...].astype(BF)


    def js(t):
        return pl.ds(0, 2) if t == 0 else pl.ds(2, 1)

    def rows_of(t, m, cnt):
        return pl.ds(m if t == 0 else m * size, cnt)

    def pair_copy(t, m, cnt):
        r = rows_of(t, m, cnt)
        return rcopy(part.at[r, 1 - k_me, js(t)], pair.at[r, js(t)], p_send.at[t], p_recv.at[t, m], partner)

    def chip_sum(t, m, cnt):
        pair_copy(t, m, cnt).wait_recv()
        for i in range(cnt):
            c = m if t == 0 else m * size + i
            for j in ((0, 1), (2,))[t]:
                chip[c, j] = (part[c, k_me, j] + pair[c, j]).astype(BF)

    def far_copy(t, m, cnt, d):
        r = rows_of(t, m, cnt)
        return rcopy(chip.at[r, js(t)], far.at[d - 1, r, js(t)], f_send.at[t, d - 1], f_recv.at[t, m, d - 1],
                     xpeer(d))

    def far_start(t, m, cnt):
        for d in range(1, chips):
            far_copy(t, m, cnt, d).start()

    def activate(t, m, cnt):
        for d in range(1, chips):
            far_copy(t, m, cnt, d).wait_recv()
        for i in range(cnt):
            values(t, m if t == 0 else m * size + i)

    def values(t, c):
        def total_of(j):
            s = part[c, k_me, j] + pair[c, j]
            for d in range(1, chips):
                s = s + far[d - 1, c, j].astype(F32)
            return s

        if t == 0:
            gate, upward = total_of(0), total_of(1)
            sigma = 1.0 / (1.0 + jnp.exp(-gate))
            live = gate * sigma
            hidden = live * upward
            slope = upward * sigma * (1.0 + gate * (1.0 - sigma))
            if total % n:
                mine = first_chunk + c >= g_me * n
                hidden, live, slope = (jnp.where(mine, v, 0.0) for v in (hidden, live, slope))
            coef[c, 0] = slope
            coef[c, 1] = live
            act[c, k_me, 0] = hidden.astype(BF)
        else:
            back = total_of(2)
            act[c, k_me, 1] = (back * coef[c, 0]).astype(BF)
            act[c, k_me, 2] = (back * coef[c, 1]).astype(BF)

    def ja(t):
        return pl.ds(0, 1) if t == 0 else pl.ds(1, 2)

    def act_copy(t, m, cnt):
        r = rows_of(t, m, cnt)
        ref = act.at[r, k_me, ja(t)]
        return rcopy(ref, ref, a_send.at[t], a_recv.at[t, m], partner)

    def act_wait(t, m, cnt):
        ref = act.at[rows_of(t, m, cnt), 1 - k_me, ja(t)]
        rcopy(ref, ref, a_send.at[t], a_recv.at[t, m], partner).wait_recv()

    def lhs(c, j):
        return jnp.concatenate([act[c, 0, j].astype(F32), act[c, 1, j].astype(F32)], axis=0).astype(BF)


    outs = [(0, PARTS), (PARTS, 2), (PARTS + 2, 1)]

    def acc_of(q):
        acc = mixed if q < PARTS else grad
        return acc, pl.ds((q % PARTS) * pw, pw)

    def run(o):
        return range(outs[o][0], sum(outs[o]))

    def y_stage(o):
        for q in run(o):
            acc, cols = acc_of(q)
            ysend[q] = acc[half:, cols].astype(BF)

    def y_copy(o):
        qs = pl.ds(*outs[o])
        return rcopy(ysend.at[qs], yrecv.at[qs], y_send.at[0], y_recv.at[o], across)

    def span(s):
        return nb >> (s + 1)

    def z_base(s):
        return nb - (nb >> s)

    def z_copy(o, s):
        at = (pl.ds(*outs[o]), pl.ds(z_base(s), span(s)))
        return rcopy(zsend.at[at], zrecv.at[at], z_send.at[s], z_recv.at[o, s], zpeer(bits[s]))

    def z_stage(o, s):
        (y_copy(o) if s == 0 else z_copy(o, s - 1)).wait_recv()
        for q in run(o):
            acc, cols = acc_of(q)
            if s == 0:
                ysum[q] = acc[:half, cols] + yrecv[q].astype(F32)
            else:
                for i in range(span(s - 1)):
                    p = i << s
                    r = pl.ds(p * rows, rows)
                    for j in range(zfold):
                        cs = pl.ds(j * zwide, zwide)
                        ysum[q, r, cs] = ysum[q, r, cs] + (
                            zrecv[q, z_base(s - 1) + i, j * rows:(j + 1) * rows, :].astype(F32))
            if s < steps:
                for i in range(span(s)):
                    p = (2 * i + 1) << s
                    for j in range(zfold):
                        zflat[q, i, j * rows:(j + 1) * rows, :] = (
                            ysum[q, p * rows:(p + 1) * rows, j * zwide:(j + 1) * zwide])
                    zsend[q, z_base(s) + i] = zflat[q, i].astype(BF)
            else:
                out[q // PARTS, :, cols] = ysum[q, :rows, :].astype(BF)

    def z_start(o, s):
        if s < steps:
            z_copy(o, s).start()

    def z_step(o, s):
        if s <= steps:
            z_stage(o, s)
            z_start(o, s)


    def last_peer(e):
        return {"grp": flip(g_me, 1) if e >= nb else g_me, "blk": flips(b_me, e % nb)}

    def last_stage():
        for e in range(1, 2 * nb):
            for j in range(zfold):
                lflat[e - 1, j * rows:(j + 1) * rows, :] = (
                    grad[e * rows:(e + 1) * rows, depth - pw + j * zwide:depth - pw + (j + 1) * zwide])
        lsend[...] = lflat[...].astype(BF)

    def last_copy(e):
        return rcopy(lsend.at[e - 1], lrecv.at[e - 1], l_send.at[0], l_recv.at[e - 1], last_peer(e))

    def last_sum():
        for e in range(1, 2 * nb):
            last_copy(e).wait_recv()
        for j in range(zfold):
            lo = depth - pw + j * zwide
            v = grad[:rows, lo:lo + zwide]
            for e in range(1, 2 * nb):
                v = v + lrecv[e - 1, j * rows:(j + 1) * rows, :].astype(F32)
            out[1, :, lo:lo + zwide] = v.astype(BF)


    def valid(c):
        return jnp.logical_and(c >= 0, c < n)

    def chunk(c, f):
        pl.when(valid(c))(lambda: f(c, 1))

    def group(m, f):
        pl.when(jnp.logical_and(m >= 0, m < n // size))(lambda: f(m, size))
        if n % size:
            pl.when(m == n // size)(lambda: f(n // size, n % size))

    def grouped(f):
        lax.fori_loop(0, n // size, lambda m, _: f(m, [m * size + i for i in range(size)]) or 0, 0)
        if n % size:
            f(jnp.int32(n // size), list(range(n - n % size, n)))

    def at(m, k, f):
        pl.when(m == min(k, groups - 1))(f)


    barrier = pltpu.get_barrier_semaphore()
    peers = [partner, across] + [zpeer(m) for m in bits] + [xpeer(d) for d in range(1, chips)]
    for where in peers:
        pl.semaphore_signal(barrier, inc=1, device_id=where, device_id_type=MESH)
    for w in range(2):
        own_copy(w).start()
    for w in range(2):
        fold_own(w)
    for c in range(n):
        for cp in load_gu(c):
            cp.start()
    for m in range(groups):
        load_d(m, m * size, min(size, n - m * size)).start()
    pl.semaphore_wait(barrier, len(peers))

    for w in range(2):
        tok_forward(w, 0)
    for e in range(1, nb):
        tok_forward(0, e)
    for e in range(1, nb - 1):
        tok_forward(1, e)
    pack(0, mixed, tok)

    def top(t):
        chunk(t - 1, lambda c, i: pair_copy(0, c, i).start())
        chunk(t - 3, lambda c, i: far_start(0, c, i))

    def bottom(t):
        chunk(t - 2, lambda c, i: chip_sum(0, c, i))

    def keep(c, j, v):
        part[c, 0, j] = v[:half]
        part[c, 1, j] = v[half:]


    soon = max(0, n - 10)

    def forward(i, _):
        top(i)
        chunk(i - n + soon, lambda c, _: activate(0, c, 1))

        @pl.when(i == min(7, n - 1))
        def _():
            tok_forward(1, nb - 1)

        wait_gu(i)
        keep(i, 0, jnp.dot(tok[...], wgu[i, 0], preferred_element_type=F32))
        keep(i, 1, jnp.dot(tok[...], wgu[i, 1], preferred_element_type=F32))
        chunk(i - n + soon, lambda c, _: act_copy(0, c, 1).start())
        bottom(i)
        return 0

    lax.fori_loop(0, n, forward, 0)
    pack(1, grad, cot)
    mixed[...] = jnp.zeros_like(mixed)
    grad[...] = jnp.zeros_like(grad)


    def b_top(m):
        group(m - 1, lambda g, i: pair_copy(1, g, i).start())
        group(m - 3, lambda g, i: far_start(1, g, i))

    def b_bottom(m):
        group(m - 2, lambda g, i: chip_sum(1, g, i))

    def hidden_of(m, do):
        for i in range(2):
            chunk(soon + 2 * m + i, do)

    def last_hidden(m, do):
        chunk(soon + 2 * groups + m, do)

    def backward(m, cs):
        @pl.when(m == 0)
        def _():
            pair_copy(0, n - 1, 1).start()
            far_start(0, n - 3, 1)

        @pl.when(m == 1)
        def _():
            far_start(0, n - 2, 1)
            far_start(0, n - 1, 1)

        b_top(m)
        hidden_of(m, lambda c, _: activate(0, c, 1))
        load_d(m, cs[0], len(cs)).wait()
        for c in cs:
            keep(c, 2, lax.dot_general(cot[...], wd_of(c), NT, preferred_element_type=F32))
        hidden_of(m, lambda c, _: act_copy(0, c, 1).start())
        @pl.when(m == 0)
        def _():
            chip_sum(0, n - 2, 1)
            chip_sum(0, n - 1, 1)

        b_bottom(m)

    grouped(backward)

    early = max(0, groups - 2)

    def mix(m, cs):
        b_top(groups + m)
        last_hidden(m, lambda c, _: activate(0, c, 1))
        group(m - (groups - early), lambda g, i: activate(1, g, i))
        for c in cs:
            act_wait(0, c, 1)
        acc = 0.0
        for c in cs:
            acc = acc + jnp.dot(lhs(c, 0), wd_of(c), preferred_element_type=F32)
        mixed[...] += acc
        last_hidden(m, lambda c, _: act_copy(0, c, 1).start())
        group(m - (groups - early), lambda g, i: act_copy(1, g, i).start())
        b_bottom(groups + m)

    grouped(mix)

    def add_grad(lo, hi, cs):
        acc = 0.0
        for c in cs:
            acc = acc + lax.dot_general(lhs(c, 1), wgu[c, 0, lo:hi, :], NT, preferred_element_type=F32)
            acc = acc + lax.dot_general(lhs(c, 2), wgu[c, 1, lo:hi, :], NT, preferred_element_type=F32)
        grad[:, lo:hi] += acc

    y_stage(0)

    def grad_a(m, cs):
        at(m, 0, lambda: y_copy(0).start())
        at(m, 3, lambda: z_stage(0, 0))
        group(m + early, lambda g, i: activate(1, g, i))
        act_wait(1, m, len(cs))
        add_grad(0, 2 * pw, cs)
        group(m + early, lambda g, i: act_copy(1, g, i).start())

    grouped(grad_a)
    z_start(0, 0)
    y_stage(1)

    def grad_b(m, cs):
        at(m, 0, lambda: y_copy(1).start())
        add_grad(2 * pw, 3 * pw, cs)

    grouped(grad_b)
    y_stage(2)

    def grad_c(m, cs):
        at(m, 0, lambda: y_copy(2).start())
        at(m, 1, lambda: z_stage(0, 1))
        at(m, 2, lambda: z_start(0, 1))
        at(m, 2, lambda: z_stage(1, 0))
        at(m, 3, lambda: z_start(1, 0))
        add_grad(3 * pw, depth, cs)

    grouped(grad_c)
    last_stage()
    z_step(2, 0)
    for e in range(2 * nb - 1, 0, -1):
        last_copy(e).start()
    z_step(1, 1)
    z_step(2, 1)
    z_step(0, 2)
    z_step(1, 2)
    z_step(2, 2)
    for s in range(3, steps + 1):
        for o in range(len(outs)):
            z_step(o, s)
    last_sum()


    def left(ref, sem):
        rcopy(ref, ref, sem, sem, across).wait_send()

    for w in range(2):
        left(got.at[w, pl.ds(1, 2 * nb - 1)], tk_send.at[w])
    for t in range(2):
        left(part.at[:, 0, js(t)], p_send.at[t])
        for d in range(1, chips):
            left(chip.at[:, js(t)], f_send.at[t, d - 1])
        left(act.at[:, 0, ja(t)], a_send.at[t])
    left(ysend, y_send.at[0])
    for s in range(steps):
        left(zsend.at[:, pl.ds(z_base(s), span(s))], z_send.at[s])
    left(lsend, l_send.at[0])


def per_device(ng, nb, nu, tokens, cotangent, gate_weight, up_weight, down_weight):
    rows, depth = tokens.shape
    width = gate_weight.shape[1]
    fc = next(w for w in (256, 128) if width % w == 0)
    total = width // fc
    n = pl.cdiv(total, ng)
    chips = nu // 2
    assert ng == 2 and nb & (nb - 1) == 0 and nb > 1 and nu % 2 == 0 and chips > 1
    assert n >= 7 and depth % (128 * PARTS) == 0 and (rows * nb) % 8 == 0
    half = rows * nb
    t = 2 * half
    pw = depth // PARTS
    steps = nb.bit_length() - 1
    fold = next((f for f in (1, 2, 4, 8) if rows * f % 8 == 0 and depth % (256 * f) == 0), 1)
    wide = depth // (2 * fold)
    zfold = next((f for f in (1, 2, 4) if rows * f % 8 == 0 and pw % (128 * f) == 0), 1)
    zwide = pw // zfold
    dma = pltpu.SemaphoreType.DMA
    vm = pltpu.VMEM
    both = pl.pallas_call(
        functools.partial(kernel, nb, nu, n, total, fc),
        out_shape=vm((2, rows, depth), BF),
        in_specs=[pl.BlockSpec(memory_space=pl.ANY)] * 5,
        out_specs=pl.BlockSpec(memory_space=pltpu.VMEM),
        scratch_shapes=[
            vm((n, 2, depth, fc), BF), vm((n * fc, depth), BF),
            vm((2, rows, depth), BF), vm((2, 2, rows * fold, wide), F32),
            vm((2, 2 * nb, 2, rows * fold, wide), BF), vm((t, depth), BF), vm((t, depth), BF),
            vm((n, 2, 3, half, fc), F32), vm((n, 3, half, fc), F32), vm((n, 3, half, fc), BF),
            vm((chips - 1, n, 3, half, fc), BF), vm((n, 2, half, fc), F32), vm((n, 2, 3, half, fc), BF),
            vm((t, depth), F32), vm((t, depth), F32),
            vm((2 * PARTS - 1, half, pw), BF), vm((2 * PARTS - 1, half, pw), BF), vm((2 * PARTS - 1, half, pw), F32),
            vm((2 * PARTS - 1, nb // 2, rows * zfold, zwide), F32),
            vm((2 * PARTS - 1, nb - 1, rows * zfold, zwide), BF), vm((2 * PARTS - 1, nb - 1, rows * zfold, zwide), BF),
            vm((2 * nb - 1, rows * zfold, zwide), F32), vm((2 * nb - 1, rows * zfold, zwide), BF),
            vm((2 * nb - 1, rows * zfold, zwide), BF),
            dma((n,)), dma((pl.cdiv(n, SIZE),)), dma((2,)), dma((2,)), dma((2, 2 * nb, 2)),
            dma((2,)), dma((2, n)), dma((2, chips - 1)), dma((2, n, chips - 1)), dma((2,)), dma((2, n)),
            dma((1,)), dma((3,)), dma((steps,)), dma((3, steps)), dma((1,)), dma((2 * nb - 1,)),
        ],
        compiler_params=pltpu.CompilerParams(
            collective_id=0, has_side_effects=True, vmem_limit_bytes=67043328 - 4 * depth * pl.cdiv(rows, 16) * 16),
    )(tokens, cotangent, gate_weight, up_weight, down_weight)
    return both[0], both[1]


def solution(mesh):
    return jax.shard_map(
        functools.partial(per_device, mesh.shape["grp"], mesh.shape["blk"], mesh.shape["bulk"]),
        mesh=mesh,
        in_specs=(
            P(("grp", "blk"), "bulk"),
            P(("grp", "blk"), "bulk"),
            P("bulk", "blk"),
            P("bulk", "blk"),
            P("blk", "bulk"),
        ),
        out_specs=(P(("grp", "blk"), "bulk"), P(("grp", "blk"), "bulk")),
        check_vma=False,
    )
```

```python
import functools

import jax
import jax.numpy as jnp
from jax import lax
from jax.experimental import pallas as pl
from jax.experimental.pallas import tpu as pltpu
from jax.sharding import PartitionSpec as P

MESH = pl.DeviceIdType.MESH
BF = jnp.bfloat16
F32 = jnp.float32
NT = (((1,), (1,)), ((), ()))
PARTS = 4
LEAD = 5
SOON = 4


def chunks_at_once(n):
    return next(s for s in (4, 2) if n // s >= 3)


def flip(i, m):
    return i + m - 2 * m * ((i // m) % 2)


def flips(i, bits):
    for s in range(bits.bit_length()):
        if bits >> s & 1:
            i = flip(i, 1 << s)
    return i


def kernel(nb, nu, n, total, fc, tok_in, cot_in, wg_hbm, wu_hbm, wd_hbm, out,
           wgu, wd, own, folded, got, tokh, tok, cot, part, pair, chip, far, coef, act,
           mixed, grad, ysend, yrecv, ysum, zflat, zsend, zrecv, lflat, lsend, lrecv,
           gu_sem, d_sem, own_sem, tk_send, tk_recv, p_send, p_recv,
           f_send, f_recv, a_send, a_recv, y_send, y_recv, z_send, z_recv, l_send, l_recv):
    g_me = lax.axis_index("grp")
    b_me = lax.axis_index("blk")
    u_me = lax.axis_index("bulk")
    x_me, k_me = u_me // 2, u_me % 2
    chips = nu // 2
    rows, depth = tok_in.shape
    half = nb * rows
    pw = depth // PARTS
    size = chunks_at_once(n)
    groups = n // size
    rest = size + n % size
    lead = min(LEAD, n - 3)
    soon = min(SOON, lead)
    steps = nb.bit_length() - 1
    bits = [1 << s for s in range(steps)]
    first_chunk = jnp.minimum(g_me * n, total - n)
    partner = {"bulk": x_me * 2 + (1 - k_me)}
    across = {"grp": 1 - g_me}

    def zpeer(m):
        return {"blk": flip(b_me, m)}

    def xpeer(d):
        return {"bulk": ((x_me + d) % chips) * 2 + k_me}

    def rcopy(src, dst, ss, rs, where):
        return pltpu.make_async_remote_copy(
            src_ref=src, dst_ref=dst, send_sem=ss, recv_sem=rs, device_id=where, device_id_type=MESH)


    def load_gu(c):
        cols = pl.ds(pl.multiple_of((first_chunk + c) * fc, fc), fc)
        return (pltpu.make_async_copy(wg_hbm.at[:, cols], wgu.at[c, 0], gu_sem.at[c]),
                pltpu.make_async_copy(wu_hbm.at[:, cols], wgu.at[c, 1], gu_sem.at[c]))

    def wait_gu(c):
        pltpu.make_async_copy(wgu.at[c], wgu.at[c], gu_sem.at[c]).wait()

    def load_d(m, c, cnt):
        src = pl.ds(pl.multiple_of((first_chunk + c) * fc, fc), cnt * fc)
        dst = pl.ds(pl.multiple_of(c * fc, fc), cnt * fc)
        return pltpu.make_async_copy(wd_hbm.at[src, :], wd.at[dst, :], d_sem.at[m])

    def wd_of(c):
        return wd[pl.ds(pl.multiple_of(c * fc, fc), fc), :]


    dims = bits[::-1] + [nb]
    fold, wide = got.shape[3] // rows, got.shape[4]
    zfold, zwide = zsend.shape[2] // rows, zsend.shape[3]

    def across_dim(m):
        return across if m == nb else zpeer(m)

    def tok_ref(w, e, h):
        return got.at[w, e, h]

    def tok_copy(w, e, m, h):
        return rcopy(tok_ref(w, e, h), tok_ref(w, e + m, h), tk_send.at[w], tk_recv.at[w, e + m, h], across_dim(m))

    def tok_wait(w, e, h):
        rcopy(tok_ref(w, e, h), tok_ref(w, e, h), tk_send.at[w], tk_recv.at[w, e, h], across).wait_recv()

    def later(e):
        last = max([i for i, m in enumerate(dims) if (e // m) % 2], default=-1)
        return dims[last + 1:]

    def tok_forward(w, e):
        if e == 0:
            for m in later(e):
                for h in range(2):
                    tok_copy(w, e, m, h).start()
        else:
            for h in range(2):
                tok_wait(w, e, h)
                for m in later(e):
                    tok_copy(w, e, m, h).start()

    def own_copy(w):
        return pltpu.make_async_copy((tok_in, cot_in)[w], own.at[w], own_sem.at[w])

    def place(h, j):
        lo = (h * fold + j) * wide
        return slice(lo, lo + wide)

    def fold_own(w):
        own_copy(w).wait()
        for h in range(2):
            for j in range(fold):
                folded[w, h, j * rows:(j + 1) * rows, :] = own[w, :, place(h, j)].astype(F32)
        got[w, 0] = folded[w].astype(BF)

    def pack(w, other, scratch):
        for e in range(other * nb, (other + 1) * nb):
            for h in range(2):
                if other:
                    tok_wait(w, e, h)
                for j in range(fold):
                    scratch[e * rows:(e + 1) * rows, place(h, j)] = (
                        got[w, e, h, j * rows:(j + 1) * rows, :].astype(F32))


    def js(t):
        return pl.ds(0, 2) if t == 0 else pl.ds(2, 1)

    def rows_of(t, m, cnt):
        return pl.ds(m if t == 0 else m * size, cnt)

    def pair_copy(t, m, cnt):
        r = rows_of(t, m, cnt)
        return rcopy(part.at[r, 1 - k_me, js(t)], pair.at[r, js(t)], p_send.at[t], p_recv.at[t, m], partner)

    def chip_sum(t, m, cnt):
        pair_copy(t, m, cnt).wait_recv()
        for i in range(cnt):
            c = m if t == 0 else m * size + i
            for j in ((0, 1), (2,))[t]:
                chip[c, j] = (part[c, k_me, j] + pair[c, j]).astype(BF)

    def far_copy(t, m, cnt, d):
        r = rows_of(t, m, cnt)
        return rcopy(chip.at[r, js(t)], far.at[d - 1, r, js(t)], f_send.at[t, d - 1], f_recv.at[t, m, d - 1],
                     xpeer(d))

    def far_start(t, m, cnt):
        for d in range(1, chips):
            far_copy(t, m, cnt, d).start()

    def activate(t, m, cnt):
        for d in range(1, chips):
            far_copy(t, m, cnt, d).wait_recv()
        for i in range(cnt):
            values(t, m if t == 0 else m * size + i)

    def values(t, c):
        def total_of(j):
            s = part[c, k_me, j] + pair[c, j]
            for d in range(1, chips):
                s = s + far[d - 1, c, j].astype(F32)
            return s

        if t == 0:
            gate, upward = total_of(0), total_of(1)
            sigma = 1.0 / (1.0 + jnp.exp(-gate))
            live = gate * sigma
            hidden = live * upward
            slope = upward * sigma * (1.0 + gate * (1.0 - sigma))
            if total % n:
                mine = first_chunk + c >= g_me * n
                hidden, live, slope = (jnp.where(mine, v, 0.0) for v in (hidden, live, slope))
            coef[c, 0] = slope
            coef[c, 1] = live
            act[c, k_me, 0] = hidden.astype(BF)
        else:
            back = total_of(2)
            act[c, k_me, 1] = (back * coef[c, 0]).astype(BF)
            act[c, k_me, 2] = (back * coef[c, 1]).astype(BF)

    def ja(t):
        return pl.ds(0, 1) if t == 0 else pl.ds(1, 2)

    def act_copy(t, m, cnt):
        r = rows_of(t, m, cnt)
        ref = act.at[r, k_me, ja(t)]
        return rcopy(ref, ref, a_send.at[t], a_recv.at[t, m], partner)

    def act_wait(t, m, cnt):
        ref = act.at[rows_of(t, m, cnt), 1 - k_me, ja(t)]
        rcopy(ref, ref, a_send.at[t], a_recv.at[t, m], partner).wait_recv()

    def lhs(c, j):
        return jnp.concatenate([act[c, 0, j].astype(F32), act[c, 1, j].astype(F32)], axis=0).astype(BF)


    outs = [(0, PARTS), (PARTS, 2), (PARTS + 2, 1)]

    def acc_of(q):
        acc = mixed if q < PARTS else grad
        return acc, pl.ds((q % PARTS) * pw, pw)

    def run(o):
        return range(outs[o][0], sum(outs[o]))

    def y_stage(o):
        for q in run(o):
            acc, cols = acc_of(q)
            ysend[q] = acc[half:, cols].astype(BF)

    def y_copy(o):
        qs = pl.ds(*outs[o])
        return rcopy(ysend.at[qs], yrecv.at[qs], y_send.at[0], y_recv.at[o], across)

    def span(s):
        return nb >> (s + 1)

    def z_base(s):
        return nb - (nb >> s)

    def z_copy(o, s):
        at = (pl.ds(*outs[o]), pl.ds(z_base(s), span(s)))
        return rcopy(zsend.at[at], zrecv.at[at], z_send.at[s], z_recv.at[o, s], zpeer(bits[s]))

    def z_stage(o, s):
        (y_copy(o) if s == 0 else z_copy(o, s - 1)).wait_recv()
        for q in run(o):
            acc, cols = acc_of(q)
            if s == 0:
                ysum[q] = acc[:half, cols] + yrecv[q].astype(F32)
            else:
                for i in range(span(s - 1)):
                    p = i << s
                    r = pl.ds(p * rows, rows)
                    for j in range(zfold):
                        cs = pl.ds(j * zwide, zwide)
                        ysum[q, r, cs] = ysum[q, r, cs] + (
                            zrecv[q, z_base(s - 1) + i, j * rows:(j + 1) * rows, :].astype(F32))
            if s < steps:
                for i in range(span(s)):
                    p = (2 * i + 1) << s
                    for j in range(zfold):
                        zflat[q, i, j * rows:(j + 1) * rows, :] = (
                            ysum[q, p * rows:(p + 1) * rows, j * zwide:(j + 1) * zwide])
                    zsend[q, z_base(s) + i] = zflat[q, i].astype(BF)
            else:
                out[q // PARTS, :, cols] = ysum[q, :rows, :].astype(BF)

    def z_start(o, s):
        if s < steps:
            z_copy(o, s).start()

    def z_step(o, s):
        if s <= steps:
            z_stage(o, s)
            z_start(o, s)


    def last_peer(e):
        return {"grp": flip(g_me, 1) if e >= nb else g_me, "blk": flips(b_me, e % nb)}

    def last_stage():
        for e in range(1, 2 * nb):
            for j in range(zfold):
                lflat[e - 1, j * rows:(j + 1) * rows, :] = (
                    grad[e * rows:(e + 1) * rows, depth - pw + j * zwide:depth - pw + (j + 1) * zwide])
        lsend[...] = lflat[...].astype(BF)

    def last_copy(e):
        return rcopy(lsend.at[e - 1], lrecv.at[e - 1], l_send.at[0], l_recv.at[e - 1], last_peer(e))

    def last_sum():
        for e in range(1, 2 * nb):
            last_copy(e).wait_recv()
        for j in range(zfold):
            lo = depth - pw + j * zwide
            v = grad[:rows, lo:lo + zwide]
            for e in range(1, 2 * nb):
                v = v + lrecv[e - 1, j * rows:(j + 1) * rows, :].astype(F32)
            out[1, :, lo:lo + zwide] = v.astype(BF)


    def valid(c):
        return jnp.logical_and(c >= 0, c < n)

    def chunk(c, f):
        pl.when(valid(c))(lambda: f(c, 1))

    def group(m, f):
        pl.when(jnp.logical_and(m >= 0, m < groups - 1))(lambda: f(m, size))
        pl.when(m == groups - 1)(lambda: f(groups - 1, rest))

    def small_then_last(m, f):
        group(jnp.where(m < groups - 1, m, jnp.where(m == groups - 1, -1, m - 1)), f)

    def grouped(f):
        lax.fori_loop(0, groups - 1, lambda m, _: f(m, [m * size + i for i in range(size)]) or 0, 0)
        f(jnp.int32(groups - 1), list(range(n - rest, n)))

    def at(m, k, f):
        pl.when(m == min(k, groups - 1))(f)


    barrier = pltpu.get_barrier_semaphore()
    peers = [partner, across] + [zpeer(m) for m in bits] + [xpeer(d) for d in range(1, chips)]
    for where in peers:
        pl.semaphore_signal(barrier, inc=1, device_id=where, device_id_type=MESH)
    for w in range(2):
        own_copy(w).start()
    for w in range(2):
        fold_own(w)
    for c in (*range(n - lead, n), *range(n - lead)):
        for cp in load_gu(c):
            cp.start()
    for m in range(groups):
        load_d(m, m * size, size if m < groups - 1 else rest).start()
    pl.semaphore_wait(barrier, len(peers))

    for w in range(2):
        tok_forward(w, 0)
    for e in range(1, nb):
        tok_forward(0, e)
    for e in range(1, nb - 1):
        tok_forward(1, e)


    def done(t, h):
        whole = t - lead
        return jnp.where(h == 0, jnp.where(t < 0, -1, jnp.where(t < lead, n - lead + t, jnp.where(t < n, whole, -1))),
                         whole)

    def top(t):
        chunk(done(t - 1, 1 - k_me), lambda c, i: pair_copy(0, c, i).start())
        chunk(done(t - 3, k_me), lambda c, i: far_start(0, c, i))

    def bottom(t):
        chunk(done(t - 2, k_me), lambda c, i: chip_sum(0, c, i))

    def keep(c, j, v):
        part[c, 0, j] = v[:half]
        part[c, 1, j] = v[half:]

    def rows_first(other, t, _):
        top(t)
        ready = t - n - lead + soon
        if other:
            chunk(ready, lambda c, _: activate(0, c, 1))
        c = t - lead if other else t + n - lead
        if not other:
            wait_gu(c)
        for j in range(2):
            part[c, other, j] = jnp.dot(tokh[other], wgu[c, j], preferred_element_type=F32)
        if other:
            chunk(ready, lambda c, _: act_copy(0, c, 1).start())
        bottom(t)
        return 0

    def forward(t, _):
        top(t)
        @pl.when(t == lead + 3)
        def _():
            tok_forward(1, nb - 1)

        i = t - lead
        wait_gu(i)
        keep(i, 0, jnp.dot(tok[...], wgu[i, 0], preferred_element_type=F32))
        keep(i, 1, jnp.dot(tok[...], wgu[i, 1], preferred_element_type=F32))
        bottom(t)
        return 0

    pack(0, 0, mixed)
    tokh[0] = mixed[:half].astype(BF)
    lax.fori_loop(0, lead, functools.partial(rows_first, 0), 0)
    pack(0, 1, mixed)
    tokh[1] = mixed[half:].astype(BF)
    tok[...] = mixed[...].astype(BF)
    lax.fori_loop(lead, n, forward, 0)
    lax.fori_loop(n, n + lead, functools.partial(rows_first, 1), 0)
    for other in range(2):
        pack(1, other, grad)
    cot[...] = grad[...].astype(BF)
    mixed[...] = jnp.zeros_like(mixed)
    grad[...] = jnp.zeros_like(grad)


    def b_top(m):
        group(m - 1, lambda g, i: pair_copy(1, g, i).start())
        small_then_last(m - 2, lambda g, i: far_start(1, g, i))

    def b_bottom(m):
        small_then_last(m - 1, lambda g, i: chip_sum(1, g, i))

    def hidden_of(m, do):
        chunk(soon + m, do)
        if soon + groups < n:
            pl.when(m == groups - 1)(lambda: do(soon + groups, 1))

    def last_hidden(m, do):
        @pl.when(m == 0)
        def _():
            for c in range(soon + groups + 1, n):
                do(c, 1)

    def backward(m, cs):
        @pl.when(m == 0)
        def _():
            top(n + lead)

        @pl.when(m == 1)
        def _():
            for t in (n + lead + 1, n + lead + 2):
                chunk(done(t - 3, k_me), lambda c, i: far_start(0, c, i))

        b_top(m)
        hidden_of(m, lambda c, _: activate(0, c, 1))
        load_d(m, cs[0], len(cs)).wait()
        for c in cs:
            keep(c, 2, lax.dot_general(cot[...], wd_of(c), NT, preferred_element_type=F32))
        hidden_of(m, lambda c, _: act_copy(0, c, 1).start())
        @pl.when(m == 0)
        def _():
            bottom(n + lead)
            bottom(n + lead + 1)

        b_bottom(m)

    grouped(backward)

    early = 1

    def mix(m, cs):
        b_top(groups + m)
        last_hidden(m, lambda c, _: activate(0, c, 1))
        group(m - (groups - early), lambda g, i: activate(1, g, i))
        for c in cs:
            act_wait(0, c, 1)
        def add(cs):
            acc = 0.0
            for c in cs:
                acc = acc + jnp.dot(lhs(c, 0), wd_of(c), preferred_element_type=F32)
            mixed[...] += acc

        add(cs[:2])
        last_hidden(m, lambda c, _: act_copy(0, c, 1).start())
        group(m - (groups - early), lambda g, i: act_copy(1, g, i).start())
        if cs[2:]:
            add(cs[2:])
        b_bottom(groups + m)

    grouped(mix)

    def add_grad(lo, hi, cs):
        acc = 0.0
        for c in cs:
            acc = acc + lax.dot_general(lhs(c, 1), wgu[c, 0, lo:hi, :], NT, preferred_element_type=F32)
            acc = acc + lax.dot_general(lhs(c, 2), wgu[c, 1, lo:hi, :], NT, preferred_element_type=F32)
        grad[:, lo:hi] += acc

    y_stage(0)

    def grad_a(m, cs):
        at(m, 0, lambda: y_copy(0).start())
        at(m, 2, lambda: z_stage(0, 0))
        group(m + early, lambda g, i: activate(1, g, i))
        act_wait(1, m, len(cs))
        add_grad(0, 2 * pw, cs[:1])
        group(m + early, lambda g, i: act_copy(1, g, i).start())
        add_grad(0, 2 * pw, cs[1:])

    grouped(grad_a)
    z_start(0, 0)
    y_stage(1)

    def grad_b(m, cs):
        at(m, 0, lambda: y_copy(1).start())
        add_grad(2 * pw, 3 * pw, cs)

    grouped(grad_b)
    y_stage(2)

    def grad_c(m, cs):
        at(m, 0, lambda: y_copy(2).start())
        at(m, 2, lambda: z_stage(1, 0))
        at(m, 2, lambda: z_stage(0, 1))
        at(m, 2, lambda: z_start(1, 0))
        at(m, 2, lambda: z_start(0, 1))
        add_grad(3 * pw, depth, cs)

    grouped(grad_c)
    last_stage()
    z_step(2, 0)
    for e in range(2 * nb - 1, 0, -1):
        last_copy(e).start()
    z_step(1, 1)
    z_step(2, 1)
    z_step(0, 2)
    z_step(1, 2)
    z_step(2, 2)
    for s in range(3, steps + 1):
        for o in range(len(outs)):
            z_step(o, s)
    last_sum()


    def left(ref, sem):
        rcopy(ref, ref, sem, sem, across).wait_send()

    for w in range(2):
        left(got.at[w, pl.ds(1, 2 * nb - 1)], tk_send.at[w])
    for t in range(2):
        left(part.at[:, 0, js(t)], p_send.at[t])
        for d in range(1, chips):
            left(chip.at[:, js(t)], f_send.at[t, d - 1])
        left(act.at[:, 0, ja(t)], a_send.at[t])
    left(ysend, y_send.at[0])
    for s in range(steps):
        left(zsend.at[:, pl.ds(z_base(s), span(s))], z_send.at[s])
    left(lsend, l_send.at[0])


def per_device(ng, nb, nu, tokens, cotangent, gate_weight, up_weight, down_weight):
    rows, depth = tokens.shape
    width = gate_weight.shape[1]
    fc = next(w for w in (256, 128) if width % w == 0)
    total = width // fc
    n = pl.cdiv(total, ng)
    chips = nu // 2
    assert ng == 2 and nb & (nb - 1) == 0 and nb > 1 and nu % 2 == 0 and chips > 1
    assert n >= 7 and depth % (128 * PARTS) == 0 and (rows * nb) % 8 == 0
    half = rows * nb
    t = 2 * half
    pw = depth // PARTS
    steps = nb.bit_length() - 1
    fold = next((f for f in (1, 2, 4, 8) if rows * f % 8 == 0 and depth % (256 * f) == 0), 1)
    wide = depth // (2 * fold)
    zfold = next((f for f in (1, 2, 4) if rows * f % 8 == 0 and pw % (128 * f) == 0), 1)
    zwide = pw // zfold
    dma = pltpu.SemaphoreType.DMA
    vm = pltpu.VMEM
    both = pl.pallas_call(
        functools.partial(kernel, nb, nu, n, total, fc),
        out_shape=vm((2, rows, depth), BF),
        in_specs=[pl.BlockSpec(memory_space=pl.ANY)] * 5,
        out_specs=pl.BlockSpec(memory_space=pltpu.VMEM),
        scratch_shapes=[
            vm((n, 2, depth, fc), BF), vm((n * fc, depth), BF),
            vm((2, rows, depth), BF), vm((2, 2, rows * fold, wide), F32),
            vm((2, 2 * nb, 2, rows * fold, wide), BF),
            vm((2, half, depth), BF), vm((t, depth), BF), vm((t, depth), BF),
            vm((n, 2, 3, half, fc), F32), vm((n, 3, half, fc), F32), vm((n, 3, half, fc), BF),
            vm((chips - 1, n, 3, half, fc), BF), vm((n, 2, half, fc), F32), vm((n, 2, 3, half, fc), BF),
            vm((t, depth), F32), vm((t, depth), F32),
            vm((2 * PARTS - 1, half, pw), BF), vm((2 * PARTS - 1, half, pw), BF), vm((2 * PARTS - 1, half, pw), F32),
            vm((2 * PARTS - 1, nb // 2, rows * zfold, zwide), F32),
            vm((2 * PARTS - 1, nb - 1, rows * zfold, zwide), BF), vm((2 * PARTS - 1, nb - 1, rows * zfold, zwide), BF),
            vm((2 * nb - 1, rows * zfold, zwide), F32), vm((2 * nb - 1, rows * zfold, zwide), BF),
            vm((2 * nb - 1, rows * zfold, zwide), BF),
            dma((n,)), dma((n // chunks_at_once(n),)), dma((2,)), dma((2,)), dma((2, 2 * nb, 2)),
            dma((2,)), dma((2, n)), dma((2, chips - 1)), dma((2, n, chips - 1)), dma((2,)), dma((2, n)),
            dma((1,)), dma((3,)), dma((steps,)), dma((3, steps)), dma((1,)), dma((2 * nb - 1,)),
        ],
        compiler_params=pltpu.CompilerParams(
            collective_id=0, has_side_effects=True, vmem_limit_bytes=67043328 - 4 * depth * pl.cdiv(rows, 16) * 16),
    )(tokens, cotangent, gate_weight, up_weight, down_weight)
    return both[0], both[1]


def solution(mesh):
    return jax.shard_map(
        functools.partial(per_device, mesh.shape["grp"], mesh.shape["blk"], mesh.shape["bulk"]),
        mesh=mesh,
        in_specs=(
            P(("grp", "blk"), "bulk"),
            P(("grp", "blk"), "bulk"),
            P("bulk", "blk"),
            P("bulk", "blk"),
            P("blk", "bulk"),
        ),
        out_specs=(P(("grp", "blk"), "bulk"), P(("grp", "blk"), "bulk")),
        check_vma=False,
    )
```

```python
import functools

import jax
import jax.numpy as jnp
from jax import lax
from jax.experimental import pallas as pl
from jax.experimental.pallas import tpu as pltpu
from jax.sharding import PartitionSpec as P

MESH = pl.DeviceIdType.MESH
BF = jnp.bfloat16
F32 = jnp.float32
NT = (((1,), (1,)), ((), ()))
PARTS = 4
LEAD = 5


def chunks_at_once(n):
    return next(s for s in (4, 2) if n // s >= 3)


def flip(i, m):
    return i + m - 2 * m * ((i // m) % 2)


def flips(i, bits):
    for s in range(bits.bit_length()):
        if bits >> s & 1:
            i = flip(i, 1 << s)
    return i


def kernel(nb, nu, n, total, fc, tok_in, cot_in, wg_hbm, wu_hbm, wd_hbm, out,
           wgu, wd, own, folded, got, tokh, tok, cot, part, pair, chip, far, coef, act,
           mixed, grad, ysend, yrecv, ysum, zflat, zsend, zrecv, lflat, lsend, lrecv,
           gu_sem, d_sem, own_sem, tk_send, tk_recv, p_send, p_recv,
           f_send, f_recv, a_send, a_recv, y_send, y_recv, z_send, z_recv, l_send, l_recv):
    g_me = lax.axis_index("grp")
    b_me = lax.axis_index("blk")
    u_me = lax.axis_index("bulk")
    x_me, k_me = u_me // 2, u_me % 2
    chips = nu // 2
    rows, depth = tok_in.shape
    half = nb * rows
    pw = depth // PARTS
    size = chunks_at_once(n)
    groups = n // size
    rest = size + n % size
    lead = min(LEAD, n - 4)
    pre = 0
    steps = nb.bit_length() - 1
    bits = [1 << s for s in range(steps)]
    first_chunk = jnp.minimum(g_me * n, total - n)
    partner = {"bulk": x_me * 2 + (1 - k_me)}
    across = {"grp": 1 - g_me}

    def zpeer(m):
        return {"blk": flip(b_me, m)}

    def xpeer(d):
        return {"bulk": ((x_me + d) % chips) * 2 + k_me}

    def rcopy(src, dst, ss, rs, where):
        return pltpu.make_async_remote_copy(
            src_ref=src, dst_ref=dst, send_sem=ss, recv_sem=rs, device_id=where, device_id_type=MESH)


    def load_gu(c):
        cols = pl.ds(pl.multiple_of((first_chunk + c) * fc, fc), fc)
        return (pltpu.make_async_copy(wg_hbm.at[:, cols], wgu.at[c, 0], gu_sem.at[c]),
                pltpu.make_async_copy(wu_hbm.at[:, cols], wgu.at[c, 1], gu_sem.at[c]))

    def wait_gu(c):
        pltpu.make_async_copy(wgu.at[c], wgu.at[c], gu_sem.at[c]).wait()

    def load_d(m, c, cnt):
        src = pl.ds(pl.multiple_of((first_chunk + c) * fc, fc), cnt * fc)
        dst = pl.ds(pl.multiple_of(c * fc, fc), cnt * fc)
        return pltpu.make_async_copy(wd_hbm.at[src, :], wd.at[dst, :], d_sem.at[m])

    def wd_of(c):
        return wd[pl.ds(pl.multiple_of(c * fc, fc), fc), :]


    dims = bits[::-1] + [nb]
    fold, wide = got.shape[3] // rows, got.shape[4]
    zfold, zwide = zsend.shape[2] // rows, zsend.shape[3]

    def across_dim(m):
        return across if m == nb else zpeer(m)

    def tok_ref(w, e, h):
        return got.at[w, e, h]

    def tok_copy(w, e, m, h):
        return rcopy(tok_ref(w, e, h), tok_ref(w, e + m, h), tk_send.at[w], tk_recv.at[w, e + m, h], across_dim(m))

    def tok_wait(w, e, h):
        rcopy(tok_ref(w, e, h), tok_ref(w, e, h), tk_send.at[w], tk_recv.at[w, e, h], across).wait_recv()

    def later(e):
        last = max([i for i, m in enumerate(dims) if (e // m) % 2], default=-1)
        return dims[last + 1:]

    def tok_forward(w, e):
        if e == 0:
            for m in later(e):
                for h in range(2):
                    tok_copy(w, e, m, h).start()
        else:
            for h in range(2):
                tok_wait(w, e, h)
                for m in later(e):
                    tok_copy(w, e, m, h).start()

    def own_copy(w):
        return pltpu.make_async_copy((tok_in, cot_in)[w], own.at[w], own_sem.at[w])

    def place(h, j):
        lo = (h * fold + j) * wide
        return slice(lo, lo + wide)

    def fold_own(w):
        own_copy(w).wait()
        for h in range(2):
            for j in range(fold):
                folded[w, h, j * rows:(j + 1) * rows, :] = own[w, :, place(h, j)].astype(F32)
        got[w, 0] = folded[w].astype(BF)

    def pack(w, other, scratch):
        for e in range(other * nb, (other + 1) * nb):
            for h in range(2):
                if other:
                    tok_wait(w, e, h)
                for j in range(fold):
                    scratch[e * rows:(e + 1) * rows, place(h, j)] = (
                        got[w, e, h, j * rows:(j + 1) * rows, :].astype(F32))


    def js(t):
        return pl.ds(0, 2) if t == 0 else pl.ds(2, 1)

    def start_of(m):
        return 0 if isinstance(m, int) and m == 0 else m * size + n % size

    def rows_of(t, m, cnt):
        return pl.ds(m if t == 0 else start_of(m), cnt)

    def pair_copy(t, m, cnt):
        r = rows_of(t, m, cnt)
        return rcopy(part.at[r, 1 - k_me, js(t)], pair.at[r, js(t)], p_send.at[t], p_recv.at[t, m], partner)

    def chip_sum(t, m, cnt):
        pair_copy(t, m, cnt).wait_recv()
        for i in range(cnt):
            c = m if t == 0 else start_of(m) + i
            for j in ((0, 1), (2,))[t]:
                chip[c, j] = (part[c, k_me, j] + pair[c, j]).astype(BF)

    def far_copy(t, m, cnt, d):
        r = rows_of(t, m, cnt)
        return rcopy(chip.at[r, js(t)], far.at[d - 1, r, js(t)], f_send.at[t, d - 1], f_recv.at[t, m, d - 1],
                     xpeer(d))

    def far_start(t, m, cnt):
        for d in range(1, chips):
            far_copy(t, m, cnt, d).start()

    def activate(t, m, cnt):
        for d in range(1, chips):
            far_copy(t, m, cnt, d).wait_recv()
        for i in range(cnt):
            values(t, m if t == 0 else start_of(m) + i)

    def values(t, c):
        def total_of(j):
            s = part[c, k_me, j] + pair[c, j]
            for d in range(1, chips):
                s = s + far[d - 1, c, j].astype(F32)
            return s

        if t == 0:
            gate, upward = total_of(0), total_of(1)
            sigma = 1.0 / (1.0 + jnp.exp(-gate))
            live = gate * sigma
            hidden = live * upward
            slope = upward * sigma * (1.0 + gate * (1.0 - sigma))
            if total % n:
                mine = first_chunk + c >= g_me * n
                hidden, live, slope = (jnp.where(mine, v, 0.0) for v in (hidden, live, slope))
            coef[c, 0] = slope
            coef[c, 1] = live
            act[c, k_me, 0] = hidden.astype(BF)
        else:
            back = total_of(2)
            act[c, k_me, 1] = (back * coef[c, 0]).astype(BF)
            act[c, k_me, 2] = (back * coef[c, 1]).astype(BF)

    def ja(t):
        return pl.ds(0, 1) if t == 0 else pl.ds(1, 2)

    def act_copy(t, m, cnt):
        r = rows_of(t, m, cnt)
        ref = act.at[r, k_me, ja(t)]
        return rcopy(ref, ref, a_send.at[t], a_recv.at[t, m], partner)

    def act_wait(t, m, cnt):
        ref = act.at[rows_of(t, m, cnt), 1 - k_me, ja(t)]
        rcopy(ref, ref, a_send.at[t], a_recv.at[t, m], partner).wait_recv()

    def lhs(c, j):
        return jnp.concatenate([act[c, 0, j].astype(F32), act[c, 1, j].astype(F32)], axis=0).astype(BF)


    outs = [(0, PARTS // 2), (PARTS // 2, PARTS // 2), (PARTS, 2)]

    def acc_of(q):
        acc = mixed if q < PARTS else grad
        return acc, pl.ds((q % PARTS) * pw, pw)

    def run(o):
        return range(outs[o][0], sum(outs[o]))

    def y_stage(o):
        for q in run(o):
            acc, cols = acc_of(q)
            ysend[q] = acc[half:, cols].astype(BF)

    def y_copy(o):
        qs = pl.ds(*outs[o])
        return rcopy(ysend.at[qs], yrecv.at[qs], y_send.at[0], y_recv.at[o], across)

    def span(s):
        return nb >> (s + 1)

    def z_base(s):
        return nb - (nb >> s)

    def z_copy(o, s):
        at = (pl.ds(*outs[o]), pl.ds(z_base(s), span(s)))
        return rcopy(zsend.at[at], zrecv.at[at], z_send.at[s], z_recv.at[o, s], zpeer(bits[s]))

    def z_stage(o, s):
        (y_copy(o) if s == 0 else z_copy(o, s - 1)).wait_recv()
        for q in run(o):
            acc, cols = acc_of(q)
            if s == 0:
                ysum[q] = acc[:half, cols] + yrecv[q].astype(F32)
            else:
                for i in range(span(s - 1)):
                    p = i << s
                    r = pl.ds(p * rows, rows)
                    for j in range(zfold):
                        cs = pl.ds(j * zwide, zwide)
                        ysum[q, r, cs] = ysum[q, r, cs] + (
                            zrecv[q, z_base(s - 1) + i, j * rows:(j + 1) * rows, :].astype(F32))
            if s < steps:
                for i in range(span(s)):
                    p = (2 * i + 1) << s
                    for j in range(zfold):
                        zflat[q, i, j * rows:(j + 1) * rows, :] = (
                            ysum[q, p * rows:(p + 1) * rows, j * zwide:(j + 1) * zwide])
                    zsend[q, z_base(s) + i] = zflat[q, i].astype(BF)
            else:
                out[q // PARTS, :, cols] = ysum[q, :rows, :].astype(BF)

    def z_start(o, s):
        if s < steps:
            z_copy(o, s).start()

    def z_step(o, s):
        if s <= steps:
            z_stage(o, s)
            z_start(o, s)


    def last_peer(e):
        return {"grp": flip(g_me, 1) if e >= nb else g_me, "blk": flips(b_me, e % nb)}

    def last_cols(d, j):
        lo = depth - (2 - d) * pw + j * zwide
        return slice(lo, lo + zwide)

    def last_stage(d):
        for e in range(1, 2 * nb):
            for j in range(zfold):
                lflat[d, e - 1, j * rows:(j + 1) * rows, :] = grad[e * rows:(e + 1) * rows, last_cols(d, j)]
        lsend[d] = lflat[d].astype(BF)

    def last_copy(d, e):
        return rcopy(lsend.at[d, e - 1], lrecv.at[d, e - 1], l_send.at[0], l_recv.at[d, e - 1], last_peer(e))

    def last_start(d):
        for e in range(2 * nb - 1, 0, -1):
            last_copy(d, e).start()

    def last_sum(d):
        for e in range(1, 2 * nb):
            last_copy(d, e).wait_recv()
        for j in range(zfold):
            v = grad[:rows, last_cols(d, j)]
            for e in range(1, 2 * nb):
                v = v + lrecv[d, e - 1, j * rows:(j + 1) * rows, :].astype(F32)
            out[1, :, last_cols(d, j)] = v.astype(BF)


    def valid(c):
        return jnp.logical_and(c >= 0, c < n)

    def chunk(c, f):
        pl.when(valid(c))(lambda: f(c, 1))

    def later_group(m, f):
        pl.when(jnp.logical_and(m >= 1, m < groups))(lambda: f(m, size))

    def grouped(f, start=0):
        if start == 0:
            f(0, list(range(rest)))
        lax.fori_loop(1, groups, lambda m, _: f(m, [start_of(m) + i for i in range(size)]) or 0, 0)

    def at(m, k, f):
        pl.when(m == min(k, groups - 1))(f)


    barrier = pltpu.get_barrier_semaphore()
    peers = [partner, across] + [zpeer(m) for m in bits] + [xpeer(d) for d in range(1, chips)]
    for where in peers:
        pl.semaphore_signal(barrier, inc=1, device_id=where, device_id_type=MESH)
    for w in range(2):
        own_copy(w).start()
    for w in range(2):
        fold_own(w)
    for c in (*range(n - lead, n), *range(n - lead)):
        for cp in load_gu(c):
            cp.start()
    for m in range(groups):
        load_d(m, start_of(m), size if m else rest).start()
    pl.semaphore_wait(barrier, len(peers))

    for w in range(2):
        tok_forward(w, 0)
    for e in range(1, nb):
        tok_forward(0, e)
    for e in range(1, nb - 1):
        tok_forward(1, e)


    def done(t, h):
        whole = t - lead
        return jnp.where(h == 0, jnp.where(t < 0, -1, jnp.where(t < lead, n - lead + t, jnp.where(t < n, whole, -1))),
                         whole)

    def top(t):
        chunk(done(t - 1, 1 - k_me), lambda c, i: pair_copy(0, c, i).start())
        chunk(done(t - 3, k_me), lambda c, i: far_start(0, c, i))

    def bottom(t):
        chunk(done(t - 2, k_me), lambda c, i: chip_sum(0, c, i))

    def keep(c, j, v):
        part[c, 0, j] = v[:half]
        part[c, 1, j] = v[half:]

    def rows_first(other, t, _):
        top(t)
        ready = jnp.where(t < n + pre, t - n, jnp.where(t < n + lead - 1, t - n + 1, -1))
        if other:
            pl.when(t == n + pre)(lambda: pair_copy(1, 0, rest).start())
            pl.when(t == n + lead - 1)(lambda: far_start(1, 0, rest))
            chunk(ready, lambda c, _: activate(0, c, 1))
        c = t - lead if other else t + n - lead
        if not other:
            wait_gu(c)
        for j in range(2):
            part[c, other, j] = jnp.dot(tokh[other], wgu[c, j], preferred_element_type=F32)
        if other:
            chunk(ready, lambda c, _: act_copy(0, c, 1).start())
            pl.when(t == n + lead - 2)(lambda: chip_sum(1, 0, rest))
        bottom(t)
        return 0

    def forward(t, _):
        top(t)
        @pl.when(t == lead)
        def _():
            tok_forward(1, nb - 1)

        i = t - lead
        wait_gu(i)
        keep(i, 0, jnp.dot(tok[...], wgu[i, 0], preferred_element_type=F32))
        keep(i, 1, jnp.dot(tok[...], wgu[i, 1], preferred_element_type=F32))
        bottom(t)
        return 0

    pack(0, 0, mixed)
    tokh[0] = mixed[:half].astype(BF)
    lax.fori_loop(0, lead, functools.partial(rows_first, 0), 0)
    pack(0, 1, mixed)
    tokh[1] = mixed[half:].astype(BF)
    tok[...] = mixed[...].astype(BF)
    lax.fori_loop(lead, n, forward, 0)
    lax.fori_loop(n, n + pre, functools.partial(rows_first, 1), 0)
    for other in range(2):
        pack(1, other, grad)
    cot[...] = grad[...].astype(BF)
    mixed[...] = jnp.zeros_like(mixed)
    grad[...] = jnp.zeros_like(grad)


    def b_top(m):
        later_group(m - 1, lambda g, i: pair_copy(1, g, i).start())
        later_group(m - 2, lambda g, i: far_start(1, g, i))

    def b_bottom(m):
        later_group(m - 1, lambda g, i: chip_sum(1, g, i))

    base = lead + 1 + 2 * (groups - 2)

    def hidden_of(m, do):
        pl.when(m == 1)(lambda: do(lead, 1))
        for i in range(2):
            pl.when(m > 1)(lambda i=i: do(lead + 1 + 2 * (m - 2) + i, 1))

    def last_hidden(m, do):
        for k, cs in enumerate((range(base, min(base + 3, n)), range(base + 3, n))):
            @pl.when(m == k)
            def _():
                for c in cs:
                    do(c, 1)

    def back_dots(m, cs):
        load_d(m, cs[0], len(cs)).wait()
        for c in cs:
            keep(c, 2, lax.dot_general(cot[...], wd_of(c), NT, preferred_element_type=F32))

    def backward(m, cs):
        @pl.when(m == 1)
        def _():
            top(n + lead)

        @pl.when(m == 2)
        def _():
            for t in (n + lead + 1, n + lead + 2):
                chunk(done(t - 3, k_me), lambda c, i: far_start(0, c, i))

        b_top(m)
        hidden_of(m, lambda c, _: activate(0, c, 1))
        back_dots(m, cs)
        hidden_of(m, lambda c, _: act_copy(0, c, 1).start())

        @pl.when(m == 1)
        def _():
            bottom(n + lead)
            bottom(n + lead + 1)

        b_bottom(m)

    activate(0, pre, 1)
    back_dots(0, list(range(rest)))
    act_copy(0, pre, 1).start()
    lax.fori_loop(n + pre, n + lead, functools.partial(rows_first, 1), 0)
    grouped(backward, 1)

    def mix(m, cs):
        b_top(groups + m)
        last_hidden(m, lambda c, _: activate(0, c, 1))
        pl.when(m == groups - 1)(lambda: activate(1, 0, rest))
        for c in cs:
            act_wait(0, c, 1)
        last_hidden(m, lambda c, _: act_copy(0, c, 1).start())
        pl.when(m == groups - 1)(lambda: act_copy(1, 0, rest).start())
        acc = 0.0
        for c in cs:
            acc = acc + jnp.dot(lhs(c, 0), wd_of(c), preferred_element_type=F32)
        mixed[...] += acc
        b_bottom(groups + m)

    grouped(mix)

    def add_grad(lo, hi, cs):
        acc = 0.0
        for c in cs:
            acc = acc + lax.dot_general(lhs(c, 1), wgu[c, 0, lo:hi, :], NT, preferred_element_type=F32)
            acc = acc + lax.dot_general(lhs(c, 2), wgu[c, 1, lo:hi, :], NT, preferred_element_type=F32)
        grad[:, lo:hi] += acc

    y_stage(0)
    y_stage(1)

    def grad_a(m, cs):
        at(m, 0, lambda: y_copy(0).start())
        at(m, 1, lambda: y_copy(1).start())
        at(m, 2, lambda: z_step(0, 0))
        later_group(m + 1, lambda g, i: activate(1, g, i))
        act_wait(1, m, len(cs))
        later_group(m + 1, lambda g, i: act_copy(1, g, i).start())
        add_grad(0, 2 * pw, cs)

    grouped(grad_a)
    y_stage(2)

    def grad_b(m, cs):
        at(m, 0, lambda: y_copy(2).start())
        at(m, 0, lambda: z_step(1, 0))
        at(m, 2, lambda: z_step(0, 1))
        add_grad(2 * pw, 3 * pw, cs)

    grouped(grad_b)
    last_stage(0)

    def grad_c(m, cs):
        at(m, 0, lambda: last_start(0))
        at(m, 1, lambda: z_step(1, 1))
        at(m, 1, lambda: z_step(2, 0))
        add_grad(3 * pw, depth, cs)

    grouped(grad_c)
    last_stage(1)
    z_stage(0, 2)
    last_start(1)
    z_step(2, 1)
    z_step(1, 2)
    last_sum(0)
    z_step(2, 2)
    for s in range(3, steps + 1):
        for o in range(len(outs)):
            z_step(o, s)
    last_sum(1)


    def left(ref, sem):
        rcopy(ref, ref, sem, sem, across).wait_send()

    for w in range(2):
        left(got.at[w, pl.ds(1, 2 * nb - 1)], tk_send.at[w])
    for t in range(2):
        left(part.at[:, 0, js(t)], p_send.at[t])
        for d in range(1, chips):
            left(chip.at[:, js(t)], f_send.at[t, d - 1])
        left(act.at[:, 0, ja(t)], a_send.at[t])
    left(ysend, y_send.at[0])
    for s in range(steps):
        left(zsend.at[:, pl.ds(z_base(s), span(s))], z_send.at[s])
    left(lsend, l_send.at[0])


def per_device(ng, nb, nu, tokens, cotangent, gate_weight, up_weight, down_weight):
    rows, depth = tokens.shape
    width = gate_weight.shape[1]
    fc = next(w for w in (256, 128) if width % w == 0)
    total = width // fc
    n = pl.cdiv(total, ng)
    chips = nu // 2
    assert ng == 2 and nb & (nb - 1) == 0 and nb > 1 and nu % 2 == 0 and chips > 1
    assert n >= 7 and depth % (128 * PARTS) == 0 and (rows * nb) % 8 == 0
    half = rows * nb
    t = 2 * half
    pw = depth // PARTS
    steps = nb.bit_length() - 1
    fold = next((f for f in (1, 2, 4, 8) if rows * f % 8 == 0 and depth % (256 * f) == 0), 1)
    wide = depth // (2 * fold)
    zfold = next((f for f in (1, 2, 4) if rows * f % 8 == 0 and pw % (128 * f) == 0), 1)
    zwide = pw // zfold
    dma = pltpu.SemaphoreType.DMA
    vm = pltpu.VMEM
    both = pl.pallas_call(
        functools.partial(kernel, nb, nu, n, total, fc),
        out_shape=vm((2, rows, depth), BF),
        in_specs=[pl.BlockSpec(memory_space=pl.ANY)] * 5,
        out_specs=pl.BlockSpec(memory_space=pltpu.VMEM),
        scratch_shapes=[
            vm((n, 2, depth, fc), BF), vm((n * fc, depth), BF),
            vm((2, rows, depth), BF), vm((2, 2, rows * fold, wide), F32),
            vm((2, 2 * nb, 2, rows * fold, wide), BF),
            vm((2, half, depth), BF), vm((t, depth), BF), vm((t, depth), BF),
            vm((n, 2, 3, half, fc), F32), vm((n, 3, half, fc), F32), vm((n, 3, half, fc), BF),
            vm((chips - 1, n, 3, half, fc), BF), vm((n, 2, half, fc), F32), vm((n, 2, 3, half, fc), BF),
            vm((t, depth), F32), vm((t, depth), F32),
            vm((PARTS + 2, half, pw), BF), vm((PARTS + 2, half, pw), BF), vm((PARTS + 2, half, pw), F32),
            vm((PARTS + 2, nb // 2, rows * zfold, zwide), F32),
            vm((PARTS + 2, nb - 1, rows * zfold, zwide), BF), vm((PARTS + 2, nb - 1, rows * zfold, zwide), BF),
            vm((2, 2 * nb - 1, rows * zfold, zwide), F32), vm((2, 2 * nb - 1, rows * zfold, zwide), BF),
            vm((2, 2 * nb - 1, rows * zfold, zwide), BF),
            dma((n,)), dma((n // chunks_at_once(n),)), dma((2,)), dma((2,)), dma((2, 2 * nb, 2)),
            dma((2,)), dma((2, n)), dma((2, chips - 1)), dma((2, n, chips - 1)), dma((2,)), dma((2, n)),
            dma((1,)), dma((3,)), dma((steps,)), dma((3, steps)), dma((1,)), dma((2, 2 * nb - 1)),
        ],
        compiler_params=pltpu.CompilerParams(
            collective_id=0, has_side_effects=True, vmem_limit_bytes=67043328 - 4 * depth * pl.cdiv(rows, 16) * 16),
    )(tokens, cotangent, gate_weight, up_weight, down_weight)
    return both[0], both[1]


def solution(mesh):
    return jax.shard_map(
        functools.partial(per_device, mesh.shape["grp"], mesh.shape["blk"], mesh.shape["bulk"]),
        mesh=mesh,
        in_specs=(
            P(("grp", "blk"), "bulk"),
            P(("grp", "blk"), "bulk"),
            P("bulk", "blk"),
            P("bulk", "blk"),
            P("blk", "bulk"),
        ),
        out_specs=(P(("grp", "blk"), "bulk"), P(("grp", "blk"), "bulk")),
        check_vma=False,
    )
```

```python
import functools

import jax
import jax.numpy as jnp
from jax import lax
from jax.experimental import pallas as pl
from jax.experimental.pallas import tpu as pltpu
from jax.sharding import PartitionSpec as P

MESH = pl.DeviceIdType.MESH
BF = jnp.bfloat16
F32 = jnp.float32
NT = (((1,), (1,)), ((), ()))
PARTS = 4
LEAD = 5


def chunks_at_once(n):
    return next(s for s in (4, 2) if n // s >= 3)


def flip(i, m):
    return i + m - 2 * m * ((i // m) % 2)


def flips(i, bits):
    for s in range(bits.bit_length()):
        if bits >> s & 1:
            i = flip(i, 1 << s)
    return i


def kernel(nb, nu, n, total, fc, tok_in, cot_in, wg_hbm, wu_hbm, wd_hbm, out,
           wgu, wd, own, folded, got, tokh, tok, cot, part, pair, chip, far, coef, act,
           mixed, grad, ysend, yrecv, ysum, zflat, zsend, zrecv, lflat, lsend, lrecv,
           gu_sem, d_sem, own_sem, tk_send, tk_recv, p_send, p_recv,
           f_send, f_recv, a_send, a_recv, y_send, y_recv, z_send, z_recv, l_send, l_recv):
    g_me = lax.axis_index("grp")
    b_me = lax.axis_index("blk")
    u_me = lax.axis_index("bulk")
    x_me, k_me = u_me // 2, u_me % 2
    chips = nu // 2
    rows, depth = tok_in.shape
    half = nb * rows
    pw = depth // PARTS
    size = chunks_at_once(n)
    groups = n // size
    rest = size + n % size
    lead = min(LEAD, n - 4)
    pre = 0
    steps = nb.bit_length() - 1
    bits = [1 << s for s in range(steps)]
    first_chunk = jnp.minimum(g_me * n, total - n)
    partner = {"bulk": x_me * 2 + (1 - k_me)}
    across = {"grp": 1 - g_me}

    def zpeer(m):
        return {"blk": flip(b_me, m)}

    def xpeer(d):
        return {"bulk": ((x_me + d) % chips) * 2 + k_me}

    def rcopy(src, dst, ss, rs, where):
        return pltpu.make_async_remote_copy(
            src_ref=src, dst_ref=dst, send_sem=ss, recv_sem=rs, device_id=where, device_id_type=MESH)


    def load_gu(c):
        cols = pl.ds(pl.multiple_of((first_chunk + c) * fc, fc), fc)
        return (pltpu.make_async_copy(wg_hbm.at[:, cols], wgu.at[c, 0], gu_sem.at[c]),
                pltpu.make_async_copy(wu_hbm.at[:, cols], wgu.at[c, 1], gu_sem.at[c]))

    def wait_gu(c):
        pltpu.make_async_copy(wgu.at[c], wgu.at[c], gu_sem.at[c]).wait()

    def load_d(m, c, cnt):
        src = pl.ds(pl.multiple_of((first_chunk + c) * fc, fc), cnt * fc)
        dst = pl.ds(pl.multiple_of(c * fc, fc), cnt * fc)
        return pltpu.make_async_copy(wd_hbm.at[src, :], wd.at[dst, :], d_sem.at[m])

    def wd_of(c):
        return wd[pl.ds(pl.multiple_of(c * fc, fc), fc), :]


    dims = bits[::-1] + [nb]
    fold, wide = got.shape[3] // rows, got.shape[4]
    zfold, zwide = zsend.shape[2] // rows, zsend.shape[3]

    def across_dim(m):
        return across if m == nb else zpeer(m)

    def tok_ref(w, e, h):
        return got.at[w, e, h]

    def tok_copy(w, e, m, h):
        return rcopy(tok_ref(w, e, h), tok_ref(w, e + m, h), tk_send.at[w], tk_recv.at[w, e + m, h], across_dim(m))

    def tok_wait(w, e, h):
        rcopy(tok_ref(w, e, h), tok_ref(w, e, h), tk_send.at[w], tk_recv.at[w, e, h], across).wait_recv()

    def later(e):
        last = max([i for i, m in enumerate(dims) if (e // m) % 2], default=-1)
        return dims[last + 1:]

    def tok_forward(w, e):
        if e == 0:
            for m in later(e):
                for h in range(2):
                    tok_copy(w, e, m, h).start()
        else:
            for h in range(2):
                tok_wait(w, e, h)
                for m in later(e):
                    tok_copy(w, e, m, h).start()

    def own_copy(w):
        return pltpu.make_async_copy((tok_in, cot_in)[w], own.at[w], own_sem.at[w])

    def place(h, j):
        lo = (h * fold + j) * wide
        return slice(lo, lo + wide)

    def fold_own(w):
        own_copy(w).wait()
        for h in range(2):
            for j in range(fold):
                folded[w, h, j * rows:(j + 1) * rows, :] = own[w, :, place(h, j)].astype(F32)
        got[w, 0] = folded[w].astype(BF)

    def pack(w, other, scratch):
        for e in range(other * nb, (other + 1) * nb):
            for h in range(2):
                if other:
                    tok_wait(w, e, h)
                for j in range(fold):
                    scratch[e * rows:(e + 1) * rows, place(h, j)] = (
                        got[w, e, h, j * rows:(j + 1) * rows, :].astype(F32))


    def js(t):
        return pl.ds(0, 2) if t == 0 else pl.ds(2, 1)

    def start_of(m):
        return 0 if isinstance(m, int) and m == 0 else m * size + n % size

    def rows_of(t, m, cnt):
        return pl.ds(m if t == 0 else start_of(m), cnt)

    def pair_copy(t, m, cnt):
        r = rows_of(t, m, cnt)
        return rcopy(part.at[r, 1 - k_me, js(t)], pair.at[r, js(t)], p_send.at[t], p_recv.at[t, m], partner)

    def chip_sum(t, m, cnt):
        pair_copy(t, m, cnt).wait_recv()
        for i in range(cnt):
            c = m if t == 0 else start_of(m) + i
            for j in ((0, 1), (2,))[t]:
                chip[c, j] = (part[c, k_me, j] + pair[c, j]).astype(BF)

    def far_copy(t, m, cnt, d):
        r = rows_of(t, m, cnt)
        return rcopy(chip.at[r, js(t)], far.at[d - 1, r, js(t)], f_send.at[t, d - 1], f_recv.at[t, m, d - 1],
                     xpeer(d))

    def far_start(t, m, cnt):
        for d in range(1, chips):
            far_copy(t, m, cnt, d).start()

    def activate(t, m, cnt):
        for d in range(1, chips):
            far_copy(t, m, cnt, d).wait_recv()
        for i in range(cnt):
            values(t, m if t == 0 else start_of(m) + i)

    def values(t, c):
        def total_of(j):
            s = part[c, k_me, j] + pair[c, j]
            for d in range(1, chips):
                s = s + far[d - 1, c, j].astype(F32)
            return s

        if t == 0:
            gate, upward = total_of(0), total_of(1)
            sigma = 1.0 / (1.0 + jnp.exp(-gate))
            live = gate * sigma
            hidden = live * upward
            slope = upward * sigma * (1.0 + gate * (1.0 - sigma))
            if total % n:
                mine = first_chunk + c >= g_me * n
                hidden, live, slope = (jnp.where(mine, v, 0.0) for v in (hidden, live, slope))
            coef[c, 0] = slope
            coef[c, 1] = live
            act[c, k_me, 0] = hidden.astype(BF)
        else:
            back = total_of(2)
            act[c, k_me, 1] = (back * coef[c, 0]).astype(BF)
            act[c, k_me, 2] = (back * coef[c, 1]).astype(BF)

    def ja(t):
        return pl.ds(0, 1) if t == 0 else pl.ds(1, 2)

    def act_copy(t, m, cnt):
        r = rows_of(t, m, cnt)
        ref = act.at[r, k_me, ja(t)]
        return rcopy(ref, ref, a_send.at[t], a_recv.at[t, m], partner)

    def act_wait(t, m, cnt):
        ref = act.at[rows_of(t, m, cnt), 1 - k_me, ja(t)]
        rcopy(ref, ref, a_send.at[t], a_recv.at[t, m], partner).wait_recv()

    def lhs(c, j):
        return jnp.concatenate([act[c, 0, j].astype(F32), act[c, 1, j].astype(F32)], axis=0).astype(BF)


    outs = [(0, PARTS // 2), (PARTS // 2, PARTS // 2), (PARTS, 2)]

    def acc_of(q):
        acc = mixed if q < PARTS else grad
        return acc, pl.ds((q % PARTS) * pw, pw)

    def run(o):
        return range(outs[o][0], sum(outs[o]))

    def y_stage(o):
        for q in run(o):
            acc, cols = acc_of(q)
            ysend[q] = acc[half:, cols].astype(BF)

    def y_copy(o):
        qs = pl.ds(*outs[o])
        return rcopy(ysend.at[qs], yrecv.at[qs], y_send.at[0], y_recv.at[o], across)

    def span(s):
        return nb >> (s + 1)

    def z_base(s):
        return nb - (nb >> s)

    def z_copy(o, s):
        at = (pl.ds(*outs[o]), pl.ds(z_base(s), span(s)))
        return rcopy(zsend.at[at], zrecv.at[at], z_send.at[s], z_recv.at[o, s], zpeer(bits[s]))

    def z_stage(o, s):
        (y_copy(o) if s == 0 else z_copy(o, s - 1)).wait_recv()
        for q in run(o):
            acc, cols = acc_of(q)
            if s == 0:
                ysum[q] = acc[:half, cols] + yrecv[q].astype(F32)
            else:
                for i in range(span(s - 1)):
                    p = i << s
                    r = pl.ds(p * rows, rows)
                    for j in range(zfold):
                        cs = pl.ds(j * zwide, zwide)
                        ysum[q, r, cs] = ysum[q, r, cs] + (
                            zrecv[q, z_base(s - 1) + i, j * rows:(j + 1) * rows, :].astype(F32))
            if s < steps:
                for i in range(span(s)):
                    p = (2 * i + 1) << s
                    for j in range(zfold):
                        zflat[q, i, j * rows:(j + 1) * rows, :] = (
                            ysum[q, p * rows:(p + 1) * rows, j * zwide:(j + 1) * zwide])
                    zsend[q, z_base(s) + i] = zflat[q, i].astype(BF)
            else:
                out[q // PARTS, :, cols] = ysum[q, :rows, :].astype(BF)

    def z_start(o, s):
        if s < steps:
            z_copy(o, s).start()

    def z_step(o, s):
        if s <= steps:
            z_stage(o, s)
            z_start(o, s)


    def last_peer(e):
        return {"grp": flip(g_me, 1) if e >= nb else g_me, "blk": flips(b_me, e % nb)}

    def last_cols(d, j):
        lo = depth - (2 - d) * pw + j * zwide
        return slice(lo, lo + zwide)

    def last_stage(d):
        for e in range(1, 2 * nb):
            for j in range(zfold):
                lflat[d, e - 1, j * rows:(j + 1) * rows, :] = grad[e * rows:(e + 1) * rows, last_cols(d, j)]
        lsend[d] = lflat[d].astype(BF)

    def last_copy(d, e):
        return rcopy(lsend.at[d, e - 1], lrecv.at[d, e - 1], l_send.at[0], l_recv.at[d, e - 1], last_peer(e))

    def last_start(d):
        for e in range(2 * nb - 1, 0, -1):
            last_copy(d, e).start()

    def last_sum(d):
        for e in range(1, 2 * nb):
            last_copy(d, e).wait_recv()
        for j in range(zfold):
            v = grad[:rows, last_cols(d, j)]
            for e in range(1, 2 * nb):
                v = v + lrecv[d, e - 1, j * rows:(j + 1) * rows, :].astype(F32)
            out[1, :, last_cols(d, j)] = v.astype(BF)


    def valid(c):
        return jnp.logical_and(c >= 0, c < n)

    def chunk(c, f):
        pl.when(valid(c))(lambda: f(c, 1))

    def later_group(m, f):
        pl.when(jnp.logical_and(m >= 1, m < groups))(lambda: f(m, size))

    def grouped(f, start=0):
        if start == 0:
            f(0, list(range(rest)))
        lax.fori_loop(1, groups, lambda m, _: f(m, [start_of(m) + i for i in range(size)]) or 0, 0)

    def at(m, k, f):
        pl.when(m == min(k, groups - 1))(f)


    barrier = pltpu.get_barrier_semaphore()
    peers = [partner, across] + [zpeer(m) for m in bits] + [xpeer(d) for d in range(1, chips)]
    for where in peers:
        pl.semaphore_signal(barrier, inc=1, device_id=where, device_id_type=MESH)
    for w in range(2):
        own_copy(w).start()
    for w in range(2):
        fold_own(w)
    for c in (*range(n - lead, n), *range(n - lead)):
        for cp in load_gu(c):
            cp.start()
    for m in range(groups):
        load_d(m, start_of(m), size if m else rest).start()
    pl.semaphore_wait(barrier, len(peers))

    for w in range(2):
        tok_forward(w, 0)
    for e in range(1, nb):
        tok_forward(0, e)
    for e in range(1, nb - 1):
        tok_forward(1, e)


    def done(t, h):
        whole = t - lead
        return jnp.where(h == 0, jnp.where(t < 0, -1, jnp.where(t < lead, n - lead + t, jnp.where(t < n, whole, -1))),
                         whole)

    def top(t):
        chunk(done(t - 1, 1 - k_me), lambda c, i: pair_copy(0, c, i).start())
        chunk(done(t - 3, k_me), lambda c, i: far_start(0, c, i))

    def bottom(t):
        chunk(done(t - 2, k_me), lambda c, i: chip_sum(0, c, i))

    def keep(c, j, v):
        part[c, 0, j] = v[:half]
        part[c, 1, j] = v[half:]

    def rows_first(other, t, _):
        top(t)
        ready = jnp.where(t < n + pre, t - n, jnp.where(t < n + lead - 1, t - n + 1, -1))
        if other:
            pl.when(t == n + pre)(lambda: pair_copy(1, 0, rest).start())
            pl.when(t == n + lead - 1)(lambda: far_start(1, 0, rest))
            chunk(ready, lambda c, _: activate(0, c, 1))
        c = t - lead if other else t + n - lead
        if not other:
            wait_gu(c)
        for j in range(2):
            part[c, other, j] = jnp.dot(tokh[other], wgu[c, j], preferred_element_type=F32)
        if other:
            chunk(ready, lambda c, _: act_copy(0, c, 1).start())
            pl.when(t == n + lead - 2)(lambda: chip_sum(1, 0, rest))
        bottom(t)
        return 0

    def forward(t, _):
        top(t)
        @pl.when(t == lead + 1)
        def _():
            tok_forward(1, nb - 1)

        i = t - lead
        wait_gu(i)
        keep(i, 0, jnp.dot(tok[...], wgu[i, 0], preferred_element_type=F32))
        keep(i, 1, jnp.dot(tok[...], wgu[i, 1], preferred_element_type=F32))
        bottom(t)
        return 0

    pack(0, 0, mixed)
    tokh[0] = mixed[:half].astype(BF)
    lax.fori_loop(0, lead, functools.partial(rows_first, 0), 0)
    pack(0, 1, mixed)
    tokh[1] = mixed[half:].astype(BF)
    tok[...] = mixed[...].astype(BF)
    lax.fori_loop(lead, n, forward, 0)
    lax.fori_loop(n, n + pre, functools.partial(rows_first, 1), 0)
    for other in range(2):
        pack(1, other, grad)
    cot[...] = grad[...].astype(BF)
    mixed[...] = jnp.zeros_like(mixed)
    grad[...] = jnp.zeros_like(grad)


    def b_top(m):
        later_group(m - 1, lambda g, i: pair_copy(1, g, i).start())
        later_group(m - 2, lambda g, i: far_start(1, g, i))

    def b_bottom(m):
        later_group(m - 1, lambda g, i: chip_sum(1, g, i))

    base = lead + 1 + 2 * (groups - 2)

    def hidden_of(m, do):
        pl.when(m == 1)(lambda: do(lead, 1))
        for i in range(2):
            pl.when(m > 1)(lambda i=i: do(lead + 1 + 2 * (m - 2) + i, 1))

    def last_hidden(m, do):
        for k, cs in enumerate((range(base + 1, min(base + 4, n)), range(base + 4, n))):
            @pl.when(m == k)
            def _():
                for c in cs:
                    do(c, 1)

    def back_dots(m, cs):
        load_d(m, cs[0], len(cs)).wait()
        for c in cs:
            keep(c, 2, lax.dot_general(cot[...], wd_of(c), NT, preferred_element_type=F32))

    def backward(m, cs):
        @pl.when(m == 1)
        def _():
            top(n + lead)

        @pl.when(m == 2)
        def _():
            for t in (n + lead + 1, n + lead + 2):
                chunk(done(t - 3, k_me), lambda c, i: far_start(0, c, i))

        b_top(m)
        hidden_of(m, lambda c, _: activate(0, c, 1))
        back_dots(m, cs)
        hidden_of(m, lambda c, _: act_copy(0, c, 1).start())

        @pl.when(m == 1)
        def _():
            bottom(n + lead)
            bottom(n + lead + 1)

        b_bottom(m)
        if base < n:
            pl.when(m == groups - 1)(lambda: activate(0, base, 1))

    activate(0, pre, 1)
    back_dots(0, list(range(rest)))
    act_copy(0, pre, 1).start()
    lax.fori_loop(n + pre, n + lead, functools.partial(rows_first, 1), 0)
    grouped(backward, 1)

    def mix(m, cs):
        b_top(groups + m)
        if base < n:
            at(m, 0, lambda: act_copy(0, base, 1).start())
        last_hidden(m, lambda c, _: activate(0, c, 1))
        pl.when(m == groups - 1)(lambda: activate(1, 0, rest))
        for c in cs:
            act_wait(0, c, 1)
        last_hidden(m, lambda c, _: act_copy(0, c, 1).start())
        pl.when(m == groups - 1)(lambda: act_copy(1, 0, rest).start())
        acc = 0.0
        for c in cs:
            acc = acc + jnp.dot(lhs(c, 0), wd_of(c), preferred_element_type=F32)
        mixed[...] += acc
        b_bottom(groups + m)

    grouped(mix)

    def add_grad(lo, hi, cs):
        acc = 0.0
        for c in cs:
            acc = acc + lax.dot_general(lhs(c, 1), wgu[c, 0, lo:hi, :], NT, preferred_element_type=F32)
            acc = acc + lax.dot_general(lhs(c, 2), wgu[c, 1, lo:hi, :], NT, preferred_element_type=F32)
        grad[:, lo:hi] += acc

    y_stage(0)
    y_stage(1)

    def grad_a(m, cs):
        at(m, 0, lambda: y_copy(0).start())
        at(m, 1, lambda: y_copy(1).start())
        later_group(m + 1, lambda g, i: activate(1, g, i))
        act_wait(1, m, len(cs))
        later_group(m + 1, lambda g, i: act_copy(1, g, i).start())
        add_grad(0, 2 * pw, cs)

    grouped(grad_a)
    y_stage(2)

    def grad_b(m, cs):
        at(m, 0, lambda: y_copy(2).start())
        at(m, 0, lambda: z_step(0, 0))
        at(m, 1, lambda: z_step(1, 0))
        add_grad(2 * pw, 3 * pw, cs)

    grouped(grad_b)
    last_stage(0)

    def grad_c(m, cs):
        at(m, 0, lambda: last_start(0))
        at(m, 1, lambda: z_step(0, 1))
        at(m, 1, lambda: z_step(2, 0))
        at(m, 2, lambda: z_step(1, 1))
        add_grad(3 * pw, depth, cs)

    grouped(grad_c)
    last_stage(1)
    last_start(1)
    z_step(2, 1)
    z_step(0, 2)
    z_step(1, 2)
    last_sum(0)
    z_step(2, 2)
    for s in range(3, steps + 1):
        for o in range(len(outs)):
            z_step(o, s)
    last_sum(1)


    def left(ref, sem):
        rcopy(ref, ref, sem, sem, across).wait_send()

    for w in range(2):
        left(got.at[w, pl.ds(1, 2 * nb - 1)], tk_send.at[w])
    for t in range(2):
        left(part.at[:, 0, js(t)], p_send.at[t])
        for d in range(1, chips):
            left(chip.at[:, js(t)], f_send.at[t, d - 1])
        left(act.at[:, 0, ja(t)], a_send.at[t])
    left(ysend, y_send.at[0])
    for s in range(steps):
        left(zsend.at[:, pl.ds(z_base(s), span(s))], z_send.at[s])
    left(lsend, l_send.at[0])


def per_device(ng, nb, nu, tokens, cotangent, gate_weight, up_weight, down_weight):
    rows, depth = tokens.shape
    width = gate_weight.shape[1]
    fc = next(w for w in (256, 128) if width % w == 0)
    total = width // fc
    n = pl.cdiv(total, ng)
    chips = nu // 2
    assert ng == 2 and nb & (nb - 1) == 0 and nb > 1 and nu % 2 == 0 and chips > 1
    assert n >= 7 and depth % (128 * PARTS) == 0 and (rows * nb) % 8 == 0
    half = rows * nb
    t = 2 * half
    pw = depth // PARTS
    steps = nb.bit_length() - 1
    fold = next((f for f in (1, 2, 4, 8) if rows * f % 8 == 0 and depth % (256 * f) == 0), 1)
    wide = depth // (2 * fold)
    zfold = next((f for f in (1, 2, 4) if rows * f % 8 == 0 and pw % (128 * f) == 0), 1)
    zwide = pw // zfold
    dma = pltpu.SemaphoreType.DMA
    vm = pltpu.VMEM
    both = pl.pallas_call(
        functools.partial(kernel, nb, nu, n, total, fc),
        out_shape=vm((2, rows, depth), BF),
        in_specs=[pl.BlockSpec(memory_space=pl.ANY)] * 5,
        out_specs=pl.BlockSpec(memory_space=pltpu.VMEM),
        scratch_shapes=[
            vm((n, 2, depth, fc), BF), vm((n * fc, depth), BF),
            vm((2, rows, depth), BF), vm((2, 2, rows * fold, wide), F32),
            vm((2, 2 * nb, 2, rows * fold, wide), BF),
            vm((2, half, depth), BF), vm((t, depth), BF), vm((t, depth), BF),
            vm((n, 2, 3, half, fc), F32), vm((n, 3, half, fc), F32), vm((n, 3, half, fc), BF),
            vm((chips - 1, n, 3, half, fc), BF), vm((n, 2, half, fc), F32), vm((n, 2, 3, half, fc), BF),
            vm((t, depth), F32), vm((t, depth), F32),
            vm((PARTS + 2, half, pw), BF), vm((PARTS + 2, half, pw), BF), vm((PARTS + 2, half, pw), F32),
            vm((PARTS + 2, nb // 2, rows * zfold, zwide), F32),
            vm((PARTS + 2, nb - 1, rows * zfold, zwide), BF), vm((PARTS + 2, nb - 1, rows * zfold, zwide), BF),
            vm((2, 2 * nb - 1, rows * zfold, zwide), F32), vm((2, 2 * nb - 1, rows * zfold, zwide), BF),
            vm((2, 2 * nb - 1, rows * zfold, zwide), BF),
            dma((n,)), dma((n // chunks_at_once(n),)), dma((2,)), dma((2,)), dma((2, 2 * nb, 2)),
            dma((2,)), dma((2, n)), dma((2, chips - 1)), dma((2, n, chips - 1)), dma((2,)), dma((2, n)),
            dma((1,)), dma((3,)), dma((steps,)), dma((3, steps)), dma((1,)), dma((2, 2 * nb - 1)),
        ],
        compiler_params=pltpu.CompilerParams(
            collective_id=0, has_side_effects=True, vmem_limit_bytes=67043328 - 4 * depth * pl.cdiv(rows, 16) * 16),
    )(tokens, cotangent, gate_weight, up_weight, down_weight)
    return both[0], both[1]


def solution(mesh):
    return jax.shard_map(
        functools.partial(per_device, mesh.shape["grp"], mesh.shape["blk"], mesh.shape["bulk"]),
        mesh=mesh,
        in_specs=(
            P(("grp", "blk"), "bulk"),
            P(("grp", "blk"), "bulk"),
            P("bulk", "blk"),
            P("bulk", "blk"),
            P("blk", "bulk"),
        ),
        out_specs=(P(("grp", "blk"), "bulk"), P(("grp", "blk"), "bulk")),
        check_vma=False,
    )
```
